32 devices in a mesh: slab: 8 (over z, y), head: 4 (over x, core).
Axes of the slice: x: 2, y: 2, z: 4, core: 2. Of those that a mesh axis runs over, the one named last changes fastest.
Arguments:
- q_raw: bfloat16 [3072, 2560], P('slab', 'head'), may hold values from -64 to 64
- k_raw: bfloat16 [12288, 2560], P('slab', 'head'), may hold values from -64 to 64
- values: bfloat16 [12288, 2560], P('slab', 'head'), may hold values from -6 to 6
- q_gain: float32 [2560], P('head'), may hold values from 0.5 to 1.5
- k_gain: float32 [2560], P('head'), may hold values from 0.5 to 1.5
- cotangent: bfloat16 [3072, 2560], P('slab', 'head'), may hold values from -6 to 6
- kept_tiles: int32 [48, 20, 12], P('slab', 'head'), may hold values from 0 to 191, as said below
Outputs:
- attn_out: bfloat16 [3072, 2560], P('slab', 'head')
- dq_normed: bfloat16 [3072, 2560], P('slab', 'head')
- dk_normed: bfloat16 [12288, 2560], P('slab', 'head')
- dv: bfloat16 [12288, 2560], P('slab', 'head')
The draws below stay inside these ranges and needn't reach their ends.
Inputs may be any that keep to these rules, and one draw needn't show every extreme that they name: kept_tiles[i, h, :] names 12 distinct key tiles. Query tile i is key tile 4 i; slab d holds query tiles d * 6 to (d + 1) * 6 - 1 and key tiles d * 24 to (d + 1) * 24 - 1. The first 10 entries lie in the query's own slab, the first of all being tile 4 i; the last 2 lie in other slabs. Over all query tiles of one slab and the heads that one index of head holds, the kept tiles of any one other slab form at most 2 distinct (tile, head) pairs; in every draw some slab is kept 2 such pairs by every other slab.
All inputs are finite; a program needn't handle non-finite values.
Results may differ from the reference program's by a relative error of at most 0.012.
The reference program's roundings to bfloat16 on the way count: a program that leaves them out, or rounds other values in their place, can miss the bound.
Values may be sent and summed in bfloat16 or wider, within the bound.
No kernel may reach another device: no remote copies, remote signals or barrier semaphores. Data moves between devices by JAX's collectives and lax.ppermute only.
A program may use at most 128 MiB of HBM per device.

```python
import math
import jax
import jax.numpy as jnp
from jax import lax

HEADS = 20
HD = 128
TILE = 64
KT_DEV = 24
NEAR = 10
FAR = 2
CAP = 2
QT_DEV = 6
KEPT = 12
QTILES = 48
KTILES = 192
QTOKENS = 3072
KTOKENS = 12288
D = 2560
N_SLAB = 8
N_HEAD = 4


def raw_field(key, row_count):
    stochastic_seeds = jax.random.split(key, 3)
    full_width = HEADS * HD
    column_ids = jnp.arange(full_width, dtype=jnp.int32)
    position = (column_ids % HD).astype(jnp.float32) / HD
    base_draw = jnp.clip(jax.random.normal(stochastic_seeds[0], (row_count, full_width), jnp.float32), -4.0, 4.0)
    jitter = jax.random.uniform(stochastic_seeds[1], (full_width,), jnp.float32, -0.15, 0.15)
    column = jnp.power(10.0, position + jitter)
    row_scale = jnp.power(10.0, jax.random.uniform(stochastic_seeds[2], (row_count, 1), jnp.float32, -1.0, 0.0))
    return base_draw * row_scale * column


def draw_q_raw(key, part):
    raw_values = raw_field(key, QTILES * TILE)
    return raw_values.astype(jnp.bfloat16)


def draw_k_raw(key, part):
    raw_values = raw_field(key, KTILES * TILE)
    return raw_values.astype(jnp.bfloat16)


def draw_kept_tiles(key, part):
    heads_dev = HEADS // N_HEAD
    entries = N_SLAB * CAP
    stochastic_seeds = jax.random.split(key, 8)
    slab_ids = jnp.arange(N_SLAB, dtype=jnp.int32)
    popular = jax.random.randint(stochastic_seeds[0], (), 0, N_SLAB)
    popularity = jax.random.randint(stochastic_seeds[1], (N_SLAB,), 0, 4)
    popularity = jnp.where(slab_ids == popular, 100, popularity)
    tile_rank = jax.random.randint(stochastic_seeds[2], (N_SLAB, N_HEAD, N_SLAB, KT_DEV), 0, 4096) * 1024 + jnp.arange(KT_DEV, dtype=jnp.int32)
    entry_tile = lax.top_k(tile_rank, CAP)[1].reshape(N_SLAB, N_HEAD, entries)
    entry_index = jnp.arange(entries, dtype=jnp.int32)
    entry_owner = entry_index // CAP
    requester = slab_ids[:, None, None]
    valid = entry_owner[None, None, :] != requester
    entry_order = entry_index[None, None, :] - jnp.where(entry_owner[None, None, :] > requester, CAP, 0)
    rotate = jax.random.randint(stochastic_seeds[3], (N_SLAB, N_HEAD, 1), 0, heads_dev)
    entry_head = (entry_order + rotate) % heads_dev
    entry_global = entry_owner[None, None, :] * KT_DEV + entry_tile
    row_shape = (N_SLAB, QT_DEV, N_HEAD, heads_dev, entries)
    level_noise = jax.random.randint(stochastic_seeds[4], row_shape, 0, 3)
    jitter = jax.random.randint(stochastic_seeds[5], row_shape, 0, 1024)
    head_ids = jnp.arange(heads_dev, dtype=jnp.int32)[None, None, None, :, None]
    allowed = valid[:, None, :, None, :] & (entry_head[:, None, :, None, :] == head_ids)
    entry_level = popularity[entry_owner][None, None, None, None, :]
    far_score = ((entry_level + level_noise) * 1024 + jitter) * 256 + entry_index
    far_score = jnp.where(allowed, far_score, -1)
    far_pick = lax.top_k(far_score, FAR)[1]
    lookup_matrix = jnp.broadcast_to(entry_global[:, None, :, None, :], row_shape)
    far_list = jnp.take_along_axis(lookup_matrix, far_pick, axis=4)
    adjacent_patches = jnp.arange(KT_DEV, dtype=jnp.int32)
    local_patches = 4 * jnp.arange(QT_DEV, dtype=jnp.int32)[None, :, None, None, None]
    closeness_reward = jnp.where(jnp.abs(adjacent_patches - local_patches) <= 4, 2, 0) + jnp.where(adjacent_patches == local_patches, 8, 0)
    adjacency_extent = (N_SLAB, QT_DEV, N_HEAD, heads_dev, KT_DEV)
    adjacency_weight = ((closeness_reward + jax.random.randint(stochastic_seeds[6], adjacency_extent, 0, 4)) * 4096 + jax.random.randint(stochastic_seeds[7], adjacency_extent, 0, 4096)) * 1024 + adjacent_patches
    near_list = lax.top_k(adjacency_weight, NEAR)[1] + slab_ids[:, None, None, None, None] * KT_DEV
    joined = jnp.concatenate((near_list, far_list), axis=4)
    return joined.reshape(N_SLAB * QT_DEV, HEADS, NEAR + FAR).astype(jnp.int32)


def shard_levels(stream_key, shape, pieces, smallest, top_value):
    level, own = 1.0, jax.random.fold_in(stream_key, 6)
    for dim, parts in pieces:
        steps = jnp.exp(jax.random.uniform(jax.random.fold_in(own, dim), (parts,), jnp.float32, smallest / len(pieces), top_value / len(pieces)))
        level = level * jnp.repeat(steps, shape[dim] // parts).reshape([-1 if axis == dim else 1 for axis in range(len(shape))])
    return level


def bell_draw(own_key, dims, deviation, most, shards=(), kind=jnp.bfloat16):
    level = shard_levels(own_key, dims, shards, -0.22, 0.18) if shards else 1.0
    values = jax.random.normal(own_key, dims, jnp.float32) * deviation * level
    return jnp.minimum(jnp.maximum(values, -most), most).astype(kind)


def setup_inputs(seed: int = 0) -> dict:
    seeds = jax.random.split(jax.random.key(seed), 8)
    return {
        "q_raw": draw_q_raw(jax.random.fold_in(seeds[7], 71), 0),
        "k_raw": draw_k_raw(jax.random.fold_in(seeds[7], 71), 0),
        "values": bell_draw(seeds[2], (KTOKENS, D), 1.0, 6.0, ((0, 8), (1, 4))),
        "q_gain": jnp.clip(1.0 + 0.1 * jax.random.normal(seeds[3], (D,), jnp.float32), 0.5, 1.5),
        "k_gain": jnp.clip(1.0 + 0.1 * jax.random.normal(seeds[4], (D,), jnp.float32), 0.5, 1.5),
        "cotangent": bell_draw(seeds[5], (QTOKENS, D), 1.0, 6.0, ((0, 8), (1, 4))),
        "kept_tiles": draw_kept_tiles(jax.random.fold_in(seeds[7], 71), 0),
    }


NORM_EPSILON = 1e-06

def normalize(raw_part, gain):
    widened = raw_part.astype(jnp.float32)
    mean_sq = lax.optimization_barrier(jnp.sum(widened * widened, axis=1, keepdims=True)) / (HEADS * HD)
    return (widened * lax.rsqrt(mean_sq + NORM_EPSILON) * gain).astype(jnp.bfloat16)

def merge_heads(stacked):
    return jnp.transpose(stacked, (1, 2, 0, 3)).reshape(stacked.shape[1] * TILE, HEADS * HD)

def reference(q_raw, k_raw, values, q_gain, k_gain, cotangent, kept_tiles):
    q_normed = normalize(q_raw, q_gain)
    k_normed = normalize(k_raw, k_gain)
    score_scale = 1.0 / math.sqrt(HD)
    query_count = kept_tiles.shape[0]
    key_count = k_raw.shape[0] // TILE

    def one_head(head_index):
        column_start = (head_index * HD).astype(jnp.int32)
        query_head = lax.dynamic_slice_in_dim(q_normed, column_start, HD, 1).reshape(query_count, TILE, HD)
        cotangent_head = lax.dynamic_slice_in_dim(cotangent, column_start, HD, 1).reshape(query_count, TILE, HD)
        key_head = lax.dynamic_slice_in_dim(k_normed, column_start, HD, 1).reshape(key_count, TILE, HD)
        value_head = lax.dynamic_slice_in_dim(values, column_start, HD, 1).reshape(key_count, TILE, HD)
        head_lists = lax.dynamic_index_in_dim(kept_tiles, head_index, 1, keepdims=False)

        def tile_step(grad_carry, inputs):
            key_grad, value_grad = grad_carry
            query_tile, cot_tile, chosen = inputs
            kept_keys = key_head[chosen].reshape(KEPT * TILE, HD)
            kept_values = value_head[chosen].reshape(KEPT * TILE, HD)
            scores = jnp.dot(query_tile, kept_keys.T, preferred_element_type=jnp.float32) * score_scale
            row_max = lax.optimization_barrier(jnp.max(scores, axis=1, keepdims=True))
            log_total = row_max + jnp.log(lax.optimization_barrier(jnp.sum(jnp.exp(scores - row_max), axis=1, keepdims=True)))
            attn_weights = jnp.exp(scores - log_total).astype(jnp.bfloat16)
            attn_tile = jnp.dot(attn_weights, kept_values, preferred_element_type=jnp.float32).astype(jnp.bfloat16)
            row_delta = lax.optimization_barrier(jnp.sum(cot_tile.astype(jnp.float32) * attn_tile.astype(jnp.float32), axis=1, keepdims=True))
            grad_weights = jnp.dot(cot_tile, kept_values.T, preferred_element_type=jnp.float32)
            dscore = (attn_weights.astype(jnp.float32) * (grad_weights - row_delta) * score_scale).astype(jnp.bfloat16)
            dquery = jnp.dot(dscore, kept_keys, preferred_element_type=jnp.float32).astype(jnp.bfloat16)
            grad_keys = jnp.dot(dscore.T, query_tile, preferred_element_type=jnp.float32).reshape(KEPT, TILE, HD)
            grad_values = jnp.dot(attn_weights.T, cot_tile, preferred_element_type=jnp.float32).reshape(KEPT, TILE, HD)
            key_grad = key_grad.at[chosen].add(grad_keys)
            value_grad = value_grad.at[chosen].add(grad_values)
            return ((key_grad, value_grad), (attn_tile, dquery))
        zero_grad = jnp.zeros((key_count, TILE, HD), jnp.float32)
        final_grads, per_tile = lax.scan(tile_step, (zero_grad, zero_grad), (query_head, cotangent_head, head_lists))
        return (per_tile[0], per_tile[1], final_grads[0].astype(jnp.bfloat16), final_grads[1].astype(jnp.bfloat16))
    head_outs, head_dq, head_dk, head_dv = lax.map(one_head, jnp.arange(HEADS, dtype=jnp.int32))
    return (merge_heads(head_outs), merge_heads(head_dq), merge_heads(head_dk), merge_heads(head_dv))
```

```python
import functools
import math

import jax
import jax.numpy as jnp
from jax import lax
from jax.experimental import pallas as pl
from jax.experimental.pallas import tpu as pltpu
from jax.sharding import PartitionSpec as P

TILE = 64
NEAR = 10
CAP = 2
HD = 128

NORM_EPSILON = 1e-06
MASKED = -1e30

VMEM = pl.BlockSpec(memory_space=pltpu.VMEM)
SMEM = pl.BlockSpec(memory_space=pltpu.SMEM)
ANY = pl.BlockSpec(memory_space=pl.ANY)
NT = (((1,), (1,)), ((), ()))
NN = (((1,), (0,)), ((), ()))
LOG2E = math.log2(math.e)


def dot(a, b, dims):
    return lax.dot_general(a, b, dims, preferred_element_type=jnp.float32)


def each(count, body):
    if count <= 16:
        for i in range(count):
            body(i)
    else:
        lax.fori_loop(0, count, lambda i, c: (body(i), c)[1], 0)


def inverse_rms(part_refs, full_width):
    total = part_refs[0][...]
    for ref in part_refs[1:]:
        total = total + ref[...]
    return lax.rsqrt(total / full_width + NORM_EPSILON).T


def pair_of(code, head_step):
    return code // head_step, code % head_step


def gather_kernel(
    full_width, head_step, parts, wanted, *refs
):
    part_refs, (gain, k_raw, values, out, k_buf, scale, sems) = refs[:parts], refs[parts:]
    slots = out.shape[0] * CAP

    def copies(s):
        tile, head = pair_of(wanted[s // CAP, s % CAP], head_step)
        rows = pl.ds(pl.multiple_of(tile * TILE, TILE), TILE)
        cols = pl.ds(pl.multiple_of(head * HD, HD), HD)
        return (
            pltpu.make_async_copy(k_raw.at[rows, cols], k_buf.at[s], sems.at[0, s]),
            pltpu.make_async_copy(
                values.at[rows, cols], out.at[s // CAP, CAP + s % CAP], sems.at[1, s]
            ),
        )

    each(slots, lambda s: [c.start() for c in copies(s)])
    inverse = inverse_rms(part_refs, full_width)
    for j in range(scale.shape[0] // HD):
        scale[j * HD : (j + 1) * HD, :] = jnp.broadcast_to(inverse[:, j : j + 1], (HD, HD))

    def normalize(s):
        for c in copies(s):
            c.wait()
        tile, head = pair_of(wanted[s // CAP, s % CAP], head_step)
        rows = pl.ds(pl.multiple_of(tile * TILE, TILE), TILE)
        out[s // CAP, s % CAP] = (
            k_buf[s].astype(jnp.float32) * scale[rows, :] * gain[pl.ds(head, 1), :]
        ).astype(jnp.bfloat16)

    each(slots, normalize)


def attend_kernel(full_width, head_step, parts, wanted, use_slot, *refs):
    part_refs = refs[:parts]
    (q_raw, k_raw, values, cot, q_gain, k_gain, mask, far,
     attn, dq, dk, dv, far_grad, kept_k, kept_v,
     kn, qn, s_scr, p_scr, ds_scr, fk_acc, fv_acc) = refs[parts:]
    head = pl.program_id(0)
    key_tokens = k_raw.shape[0]
    query_tokens = q_raw.shape[0]
    key_tiles = key_tokens // TILE
    pairs = query_tokens // HD
    score_scale = 1.0 / math.sqrt(HD)
    slots = far.shape[0] * CAP

    inverse = inverse_rms(part_refs, full_width)
    for j in range(key_tokens // HD):
        rows = slice(j * HD, (j + 1) * HD)
        kn[rows, :] = (
            k_raw[rows, :].astype(jnp.float32) * inverse[:, j : j + 1] * k_gain[0]
        ).astype(jnp.bfloat16)
    first = key_tokens // HD
    for j in range(pairs):
        rows = slice(j * HD, (j + 1) * HD)
        qn[rows, :] = (
            q_raw[rows, :].astype(jnp.float32) * inverse[:, first + j : first + j + 1] * q_gain[0]
        ).astype(jnp.bfloat16)

    @pl.when(head == 0)
    def _():
        fk_acc[...] = jnp.zeros_like(fk_acc)
        fv_acc[...] = jnp.zeros_like(fv_acc)

    left = lax.broadcasted_iota(jnp.int32, (2 * TILE, HD), 1) < TILE
    exponent = score_scale * LOG2E

    def far_tiles(p, kind):
        tiles = []
        for i in (2 * p, 2 * p + 1):
            for f in range(CAP):
                s = use_slot[i, head * CAP + f]
                tiles.append(far[s // CAP, kind * CAP + s % CAP])
        return jnp.concatenate(tiles, axis=0)

    def pick(x):
        return jnp.where(left, x[: 2 * TILE], x[2 * TILE :])

    def spread(x):
        zero = jnp.zeros_like(x)
        return jnp.concatenate((jnp.where(left, x, zero), jnp.where(left, zero, x)), axis=0)

    top = None
    for t in range(key_tiles):
        rows = slice(t * TILE, (t + 1) * TILE)
        block = dot(kn[rows, :], qn[...], NT) * exponent + mask[0, t : t + 1, :]
        s_scr[rows, :] = block
        block = jnp.max(block, axis=0, keepdims=True)
        top = block if top is None else jnp.maximum(top, block)

    for p in range(pairs):
        cols = slice(p * HD, (p + 1) * HD)
        q_p = qn[cols, :]
        c_p = cot[cols, :]
        far_k = far_tiles(p, 0)
        far_v = far_tiles(p, 1)
        far_s = pick(dot(far_k, q_p, NT)) * exponent
        peak = jnp.maximum(top[:, cols], jnp.max(far_s, axis=0, keepdims=True))
        far_e = jnp.exp2(far_s - peak)
        total = jnp.sum(far_e, axis=0, keepdims=True)
        for t in range(key_tiles):
            rows = slice(t * TILE, (t + 1) * TILE)
            e = jnp.exp2(s_scr[rows, cols] - peak)
            s_scr[rows, cols] = e
            total = total + jnp.sum(e, axis=0, keepdims=True)
        norm = 1.0 / total
        for t in range(key_tiles):
            rows = slice(t * TILE, (t + 1) * TILE)
            p_scr[rows, cols] = (s_scr[rows, cols] * norm).astype(jnp.bfloat16)
        far_p = (far_e * norm).astype(jnp.bfloat16)
        far_p4 = spread(far_p)
        out_t = dot(values[...].T, p_scr[:, cols], NN) + dot(far_v.T, far_p4, NN)
        out_b = out_t.astype(jnp.bfloat16)
        attn[cols, :] = out_b.T
        delta = jnp.sum(
            c_p.T.astype(jnp.float32) * out_b.astype(jnp.float32), axis=0, keepdims=True
        )
        far_dp = pick(dot(far_v, c_p, NT))
        far_ds = (far_p.astype(jnp.float32) * (far_dp - delta) * score_scale).astype(jnp.bfloat16)
        far_ds4 = spread(far_ds)
        grad_k = dot(far_ds4, q_p, NN)
        grad_v = dot(far_p4, c_p, NN)
        b = 0
        for i in (2 * p, 2 * p + 1):
            for f in range(CAP):
                s = use_slot[i, head * CAP + f]
                fk_acc[s] += grad_k[b * TILE : (b + 1) * TILE]
                fv_acc[s] += grad_v[b * TILE : (b + 1) * TILE]
                b += 1
        for t in range(key_tiles):
            rows = slice(t * TILE, (t + 1) * TILE)
            dp = dot(values[rows, :], c_p, NT)
            ds_scr[rows, cols] = (
                p_scr[rows, cols].astype(jnp.float32) * (dp - delta) * score_scale
            ).astype(jnp.bfloat16)
        dq_t = dot(kn[...].T, ds_scr[:, cols], NN) + dot(far_k.T, far_ds4, NN)
        dq[cols, :] = dq_t.astype(jnp.bfloat16).T

    grad_k = dot(ds_scr[...], qn[...], NN)
    grad_v = dot(p_scr[...], cot[...], NN)
    dk[...] = grad_k.astype(jnp.bfloat16)
    dv[...] = grad_v.astype(jnp.bfloat16)
    s_scr[:, :HD] = grad_k
    s_scr[:, HD : 2 * HD] = grad_v

    def keep(s):
        tile, owner = pair_of(wanted[s // CAP, s % CAP], head_step)

        @pl.when(owner == head)
        def _():
            rows = pl.ds(pl.multiple_of(tile * TILE, TILE), TILE)
            kept_k[s] = s_scr[rows, :HD]
            kept_v[s] = s_scr[rows, HD : 2 * HD]

    each(slots, keep)

    @pl.when(head == pl.num_programs(0) - 1)
    def _():
        def send(s):
            far_grad[s // CAP, s % CAP] = fk_acc[s].astype(jnp.bfloat16)
            far_grad[s // CAP, CAP + s % CAP] = fv_acc[s].astype(jnp.bfloat16)

        each(slots, send)


def finish_kernel(head_step, wanted, back, kept_k, kept_v, dk_in, dv_in, dk, dv,
                  acc_k, acc_v, out_k, out_v, sems):
    del dk_in, dv_in
    slots = back.shape[0] * CAP
    acc_k[...] = kept_k[...]
    acc_v[...] = kept_v[...]

    def add(s):
        code = wanted[s // CAP, s % CAP]

        def earlier(r, found):
            r = s - 1 - r
            return jnp.where(wanted[r // CAP, r % CAP] == code, r, found)

        slot = s
        if isinstance(s, int):
            for r in range(s):
                slot = earlier(r, slot)
        else:
            slot = lax.fori_loop(0, s, earlier, s)
        acc_k[slot] += back[s // CAP, s % CAP].astype(jnp.float32)
        acc_v[slot] += back[s // CAP, CAP + s % CAP].astype(jnp.float32)
        return slot

    def copies(s):
        tile, head = pair_of(wanted[s // CAP, s % CAP], head_step)
        rows = pl.ds(pl.multiple_of(tile * TILE, TILE), TILE)
        cols = pl.ds(pl.multiple_of(head * HD, HD), HD)
        return (
            pltpu.make_async_copy(out_k.at[s], dk.at[rows, cols], sems.at[0, s]),
            pltpu.make_async_copy(out_v.at[s], dv.at[rows, cols], sems.at[1, s]),
        )

    def first_of(s):
        code = wanted[s // CAP, s % CAP]

        def earlier(r, found):
            return jnp.where(wanted[r // CAP, r % CAP] == code, True, found)

        found = jnp.bool_(False)
        if isinstance(s, int):
            for r in range(s):
                found = earlier(r, found)
        else:
            found = lax.fori_loop(0, s, earlier, found)
        return jnp.logical_not(found)

    each(slots, add)
    out_k[...] = acc_k[...].astype(jnp.bfloat16)
    out_v[...] = acc_v[...].astype(jnp.bfloat16)

    def start(s):
        @pl.when(first_of(s))
        def _():
            for c in copies(s):
                c.start()

    def finish(s):
        @pl.when(first_of(s))
        def _():
            for c in copies(s):
                c.wait()

    each(slots, start)
    each(slots, finish)


def local(q_raw, k_raw, values, q_gain, k_gain, cotangent, kept_tiles):
    slab_count = lax.axis_size("slab")
    group_count = lax.axis_size("head")
    own_slab = lax.axis_index("slab")
    query_tiles, head_count, kept_count = kept_tiles.shape
    local_width = q_raw.shape[1]
    key_tiles = k_raw.shape[0] // TILE
    query_tokens, key_tokens = q_raw.shape[0], k_raw.shape[0]
    full_width = local_width * group_count
    head_step = pl.next_power_of_2(head_count)
    slots = slab_count * CAP
    vmem = pltpu.CompilerParams(vmem_limit_bytes=56 << 20)

    head_ids = jnp.arange(head_count, dtype=jnp.int32)[None, :, None]
    far_global = kept_tiles[:, :, NEAR:]
    far_owner = far_global // key_tiles
    code = far_global % key_tiles * head_step + head_ids
    slab_ids = jnp.arange(slab_count, dtype=jnp.int32)
    mine = far_owner.reshape(1, -1) == slab_ids[:, None]
    flat = code.reshape(1, -1)
    low = jnp.min(jnp.where(mine, flat, 1 << 20), axis=1)
    high = jnp.max(jnp.where(mine, flat, 0), axis=1)
    low = jnp.where(low == 1 << 20, 0, low)
    lane = jnp.arange(HD, dtype=jnp.int32)[None, :]
    request = jnp.where(lane == 0, low[:, None], high[:, None])
    wanted = lax.all_to_all(request, "slab", split_axis=0, concat_axis=0, tiled=True)
    use_slot = far_owner * CAP + (code != low[far_owner]).astype(jnp.int32)
    use_slot = use_slot.reshape(query_tiles, head_count * (kept_count - NEAR))

    k_sum = jnp.sum(jnp.square(k_raw.astype(jnp.float32)), axis=1)
    q_sum = jnp.sum(jnp.square(q_raw.astype(jnp.float32)), axis=1)
    stat_rows = -(-(key_tokens + query_tokens) // (8 * HD)) * 8
    pad = stat_rows * HD - key_tokens - query_tokens
    stats = jnp.concatenate((k_sum, q_sum, jnp.zeros((pad,), jnp.float32))).reshape(stat_rows, HD)
    parts = [stats]
    for step in range(1, group_count):
        parts.append(
            lax.ppermute(
                stats, "head", [(i, (i + step) % group_count) for i in range(group_count)]
            )
        )

    outgoing = pl.pallas_call(
        functools.partial(gather_kernel, full_width, head_step, group_count),
        out_shape=jax.ShapeDtypeStruct((slab_count, 2 * CAP, TILE, HD), jnp.bfloat16),
        in_specs=[SMEM] + [VMEM] * group_count + [VMEM, ANY, ANY],
        out_specs=VMEM,
        scratch_shapes=[
            pltpu.VMEM((slots, TILE, HD), jnp.bfloat16),
            pltpu.VMEM((key_tokens, HD), jnp.float32),
            pltpu.SemaphoreType.DMA((2, slots)),
        ],
        compiler_params=vmem,
        name="gather_far",
    )(wanted, *parts, k_gain.reshape(head_count, HD), k_raw, values)
    far = lax.all_to_all(outgoing, "slab", split_axis=0, concat_axis=0, tiled=True)

    near = kept_tiles[:, :, :NEAR] - own_slab * key_tiles
    tile_ids = jnp.arange(key_tiles, dtype=jnp.int32)
    kept = jnp.any(near[:, :, :, None] == tile_ids, axis=2)
    mask = jnp.where(kept, 0.0, MASKED).astype(jnp.float32).transpose(1, 2, 0)
    mask = jnp.repeat(mask, TILE, axis=2)

    def column(tokens):
        return pl.BlockSpec((tokens, HD), lambda h, *_: (0, h))

    def whole(*shape):
        return pl.BlockSpec(shape, lambda h, *_: (0,) * len(shape))

    gain_spec = pl.BlockSpec((1, 1, HD), lambda h, *_: (h, 0, 0))
    attn_out, dq_normed, dk, dv, far_grad, kept_k, kept_v = pl.pallas_call(
        functools.partial(attend_kernel, full_width, head_step, group_count),
        grid_spec=pltpu.PrefetchScalarGridSpec(
            num_scalar_prefetch=2,
            grid=(head_count,),
            in_specs=[whole(stat_rows, HD)] * group_count
            + [
                column(query_tokens),
                column(key_tokens),
                column(key_tokens),
                column(query_tokens),
                gain_spec,
                gain_spec,
                pl.BlockSpec((1, key_tiles, query_tokens), lambda h, *_: (h, 0, 0)),
                whole(slab_count, 2 * CAP, TILE, HD),
            ],
            out_specs=[
                column(query_tokens),
                column(query_tokens),
                column(key_tokens),
                column(key_tokens),
                whole(slab_count, 2 * CAP, TILE, HD),
                whole(slots, TILE, HD),
                whole(slots, TILE, HD),
            ],
            scratch_shapes=[
                pltpu.VMEM((key_tokens, HD), jnp.bfloat16),
                pltpu.VMEM((query_tokens, HD), jnp.bfloat16),
                pltpu.VMEM((key_tokens, query_tokens), jnp.float32),
                pltpu.VMEM((key_tokens, query_tokens), jnp.bfloat16),
                pltpu.VMEM((key_tokens, query_tokens), jnp.bfloat16),
                pltpu.VMEM((slots, TILE, HD), jnp.float32),
                pltpu.VMEM((slots, TILE, HD), jnp.float32),
            ],
        ),
        out_shape=[
            jax.ShapeDtypeStruct((query_tokens, local_width), jnp.bfloat16),
            jax.ShapeDtypeStruct((query_tokens, local_width), jnp.bfloat16),
            jax.ShapeDtypeStruct((key_tokens, local_width), jnp.bfloat16),
            jax.ShapeDtypeStruct((key_tokens, local_width), jnp.bfloat16),
            jax.ShapeDtypeStruct((slab_count, 2 * CAP, TILE, HD), jnp.bfloat16),
            jax.ShapeDtypeStruct((slots, TILE, HD), jnp.float32),
            jax.ShapeDtypeStruct((slots, TILE, HD), jnp.float32),
        ],
        compiler_params=vmem,
        name="attend",
    )(
        wanted, use_slot, *parts, q_raw, k_raw, values, cotangent,
        q_gain.reshape(head_count, 1, HD), k_gain.reshape(head_count, 1, HD), mask, far,
    )

    back = lax.all_to_all(far_grad, "slab", split_axis=0, concat_axis=0, tiled=True)
    dk, dv = pl.pallas_call(
        functools.partial(finish_kernel, head_step),
        out_shape=[jax.ShapeDtypeStruct((key_tokens, local_width), jnp.bfloat16)] * 2,
        in_specs=[SMEM, VMEM, VMEM, VMEM, ANY, ANY],
        out_specs=[ANY, ANY],
        scratch_shapes=[
            pltpu.VMEM((slots, TILE, HD), jnp.float32),
            pltpu.VMEM((slots, TILE, HD), jnp.float32),
            pltpu.VMEM((slots, TILE, HD), jnp.bfloat16),
            pltpu.VMEM((slots, TILE, HD), jnp.bfloat16),
            pltpu.SemaphoreType.DMA((2, slots)),
        ],
        input_output_aliases={4: 0, 5: 1},
        compiler_params=vmem,
        name="finish",
    )(wanted, back, kept_k, kept_v, dk, dv)
    return attn_out, dq_normed, dk, dv


def solution(mesh):
    tokens = P("slab", "head")
    return jax.shard_map(
        local,
        mesh=mesh,
        in_specs=(tokens, tokens, tokens, P("head"), P("head"), tokens, P("slab", "head", None)),
        out_specs=(tokens, tokens, tokens, tokens),
        check_vma=False,
    )
```

```python
import functools
import math

import jax
import jax.numpy as jnp
from jax import lax
from jax.experimental import pallas as pl
from jax.experimental.pallas import tpu as pltpu
from jax.sharding import PartitionSpec as P

TILE = 64
NEAR = 10
CAP = 2
HD = 128

NORM_EPSILON = 1e-06
MASKED = -1e30

VMEM = pl.BlockSpec(memory_space=pltpu.VMEM)
SMEM = pl.BlockSpec(memory_space=pltpu.SMEM)
ANY = pl.BlockSpec(memory_space=pl.ANY)
NT = (((1,), (1,)), ((), ()))
NN = (((1,), (0,)), ((), ()))
LOG2E = math.log2(math.e)


def dot(a, b, dims):
    return lax.dot_general(a, b, dims, preferred_element_type=jnp.float32)


def each(count, body):
    if count <= 16:
        for i in range(count):
            body(i)
    else:
        lax.fori_loop(0, count, lambda i, c: (body(i), c)[1], 0)


def inverse_rms(part_refs, full_width):
    total = part_refs[0][...]
    for ref in part_refs[1:]:
        total = total + ref[...]
    return lax.rsqrt(total / full_width + NORM_EPSILON).T


def pair_of(code, head_step):
    return code // head_step, code % head_step


def gather_kernel(
    full_width, head_step, parts, wanted, *refs
):
    part_refs, (gain, k_raw, values, out, k_buf, scale, sems) = refs[:parts], refs[parts:]
    slots = out.shape[0] * CAP

    def copies(s):
        tile, head = pair_of(wanted[s // CAP, s % CAP], head_step)
        rows = pl.ds(pl.multiple_of(tile * TILE, TILE), TILE)
        cols = pl.ds(pl.multiple_of(head * HD, HD), HD)
        return (
            pltpu.make_async_copy(k_raw.at[rows, cols], k_buf.at[s], sems.at[0, s]),
            pltpu.make_async_copy(
                values.at[rows, cols], out.at[s // CAP, CAP + s % CAP], sems.at[1, s]
            ),
        )

    each(slots, lambda s: [c.start() for c in copies(s)])
    inverse = inverse_rms(part_refs, full_width)
    for j in range(scale.shape[0] // HD):
        scale[j * HD : (j + 1) * HD, :] = jnp.broadcast_to(inverse[:, j : j + 1], (HD, HD))

    def normalize(s):
        for c in copies(s):
            c.wait()
        tile, head = pair_of(wanted[s // CAP, s % CAP], head_step)
        rows = pl.ds(pl.multiple_of(tile * TILE, TILE), TILE)
        out[s // CAP, s % CAP] = (
            k_buf[s].astype(jnp.float32) * scale[rows, :] * gain[pl.ds(head, 1), :]
        ).astype(jnp.bfloat16)

    each(slots, normalize)


def left_half():
    return lax.broadcasted_iota(jnp.int32, (2 * TILE, HD), 1) < TILE


def pick(x):
    return jnp.where(left_half(), x[: 2 * TILE], x[2 * TILE :])


def spread(x):
    x = x.astype(jnp.float32)
    zero = jnp.zeros_like(x)
    left = left_half()
    return jnp.concatenate(
        (jnp.where(left, x, zero), jnp.where(left, zero, x)), axis=0
    ).astype(jnp.bfloat16)


def slots_of(use_slot, head, p):
    return [use_slot[i, head * CAP + f] for i in (2 * p, 2 * p + 1) for f in range(CAP)]


def far_tiles(far, slots, kind):
    return jnp.concatenate([far[s // CAP, kind * CAP + s % CAP] for s in slots], axis=0)


def near_kernel(full_width, parts, *refs):
    part_refs = refs[:parts]
    (q_raw, k_raw, values, cot, q_gain, k_gain, mask,
     qn, kn_t, v_t, cot_t, exps, stat, kn) = refs[parts:]
    key_tokens = k_raw.shape[0]
    query_tokens = q_raw.shape[0]
    exponent = LOG2E / math.sqrt(HD)

    inverse = inverse_rms(part_refs, full_width)
    first = key_tokens // HD
    for j in range(query_tokens // HD):
        rows = slice(j * HD, (j + 1) * HD)
        qn[rows, :] = (
            q_raw[rows, :].astype(jnp.float32) * inverse[:, first + j : first + j + 1] * q_gain[0]
        ).astype(jnp.bfloat16)
    for j in range(key_tokens // HD):
        rows = slice(j * HD, (j + 1) * HD)
        kn[rows, :] = (
            k_raw[rows, :].astype(jnp.float32) * inverse[:, j : j + 1] * k_gain[0]
        ).astype(jnp.bfloat16)

    step = 4 * TILE
    top = None
    for c in range(0, key_tokens, step):
        block = dot(kn[c : c + step, :], qn[...], NT) * exponent
        for t in range(step // TILE):
            rows = slice(c + t * TILE, c + (t + 1) * TILE)
            tile = block[t * TILE : (t + 1) * TILE] + mask[0, c // TILE + t, :][None]
            exps[0, rows, :] = tile
            tile = jnp.max(tile.reshape(TILE // 8, 8, query_tokens), axis=0)
            top = tile if top is None else jnp.maximum(top, tile)
    top = jnp.max(top, axis=0, keepdims=True)
    total = jnp.zeros((8, query_tokens), jnp.float32)
    for c in range(0, key_tokens, TILE):
        e = jnp.exp2(exps[0, c : c + TILE, :] - top)
        exps[0, c : c + TILE, :] = e
        total = total + jnp.sum(e.reshape(TILE // 8, 8, query_tokens), axis=0)
    stat[0, 0:1, :] = top
    stat[0, 1:2, :] = jnp.sum(total, axis=0, keepdims=True)
    kn_t[0] = kn[...].T
    v_t[0] = values[...].T
    cot_t[0] = cot[...].T


def meet_kernel(use_slot, exps, stat, v_t, cot_t, cot, qn, far,
                attn, probs, delta_out, far_ds_out, far_grad, fk_acc, fv_acc):
    head = pl.program_id(0)
    key_tokens, query_tokens = exps.shape[1:]
    pairs = query_tokens // HD
    score_scale = 1.0 / math.sqrt(HD)
    slots = far.shape[0] * CAP

    @pl.when(head == 0)
    def _():
        fk_acc[...] = jnp.zeros_like(fk_acc)
        fv_acc[...] = jnp.zeros_like(fv_acc)

    far_v, far_e, used = [], [], []
    scales = []
    for p in range(pairs):
        cols = slice(p * HD, (p + 1) * HD)
        used.append(slots_of(use_slot, head, p))
        far_v.append(far_tiles(far, used[p], 1))
        far_s = pick(dot(far_tiles(far, used[p], 0), qn[cols, :], NT)) * (score_scale * LOG2E)
        near_top = stat[0, 0:1, cols]
        top = jnp.maximum(near_top, jnp.max(far_s, axis=0, keepdims=True))
        e = jnp.exp2(far_s - top)
        shrink = jnp.exp2(near_top - top)
        norm = 1.0 / (stat[0, 1:2, cols] * shrink + jnp.sum(e, axis=0, keepdims=True))
        scales.append(shrink * norm)
        far_e.append((e * norm).astype(jnp.bfloat16))
    scale = jnp.concatenate(scales, axis=1)
    for c in range(0, key_tokens, TILE):
        probs[0, c : c + TILE, :] = (exps[0, c : c + TILE, :] * scale).astype(jnp.bfloat16)
    out_t = dot(v_t[0], probs[0], NN)
    for p in range(pairs):
        cols = slice(p * HD, (p + 1) * HD)
        c_p = cot[cols, :]
        far_p4 = spread(far_e[p])
        out_b = (out_t[:, cols] + dot(far_v[p].T, far_p4, NN)).astype(jnp.bfloat16)
        attn[cols, :] = out_b.T
        delta = jnp.sum(
            cot_t[0, :, cols].astype(jnp.float32) * out_b.astype(jnp.float32),
            axis=0, keepdims=True,
        )
        delta_out[0, 0:1, cols] = delta
        far_dp = pick(dot(far_v[p], c_p, NT))
        far_ds = (far_e[p].astype(jnp.float32) * (far_dp - delta) * score_scale).astype(jnp.bfloat16)
        far_ds_out[0, :, cols] = far_ds
        grad_k = dot(spread(far_ds), qn[cols, :], NN)
        grad_v = dot(far_p4, c_p, NN)
        for b, s in enumerate(used[p]):
            fk_acc[s] += grad_k[b * TILE : (b + 1) * TILE]
            fv_acc[s] += grad_v[b * TILE : (b + 1) * TILE]

    @pl.when(head == pl.num_programs(0) - 1)
    def _():
        def send(s):
            far_grad[s // CAP, s % CAP] = fk_acc[s].astype(jnp.bfloat16)
            far_grad[s // CAP, CAP + s % CAP] = fv_acc[s].astype(jnp.bfloat16)

        each(slots, send)


def grad_kernel(head_step, wanted, use_slot, kn_t, qn, values, cot, probs, delta, far_ds, far,
                dq, dk, dv, kept_k, kept_v, ds, acc_k, acc_v):
    head = pl.program_id(0)
    key_tokens, query_tokens = probs.shape[1:]
    score_scale = 1.0 / math.sqrt(HD)
    slots = far.shape[0] * CAP
    step = 4 * TILE
    for c in range(0, key_tokens, step):
        rows = slice(c, c + step)
        dp = dot(values[rows, :], cot[...], NT)
        ds[rows, :] = (
            probs[0, rows, :].astype(jnp.float32) * (dp - delta[0, 0:1, :]) * score_scale
        ).astype(jnp.bfloat16)
        grad_v = dot(probs[0, rows, :], cot[...], NN)
        grad_k = dot(ds[rows, :], qn[...], NN)
        acc_k[rows, :] = grad_k
        acc_v[rows, :] = grad_v
        dk[rows, :] = grad_k.astype(jnp.bfloat16)
        dv[rows, :] = grad_v.astype(jnp.bfloat16)
    dq_t = dot(kn_t[0], ds[...], NN)
    for p in range(query_tokens // HD):
        cols = slice(p * HD, (p + 1) * HD)
        far_k = far_tiles(far, slots_of(use_slot, head, p), 0)
        part = dq_t[:, cols] + dot(far_k.T, spread(far_ds[0, :, cols]), NN)
        dq[cols, :] = part.astype(jnp.bfloat16).T

    def keep(s):
        tile, owner = pair_of(wanted[s // CAP, s % CAP], head_step)

        @pl.when(owner == head)
        def _():
            rows = pl.ds(pl.multiple_of(tile * TILE, TILE), TILE)
            kept_k[s] = acc_k[rows, :]
            kept_v[s] = acc_v[rows, :]

    each(slots, keep)


def finish_kernel(head_step, wanted, back, kept_k, kept_v, dk_in, dv_in, dk, dv,
                  acc_k, acc_v, out_k, out_v, sems):
    del dk_in, dv_in
    slots = back.shape[0] * CAP
    acc_k[...] = kept_k[...]
    acc_v[...] = kept_v[...]

    def add(s):
        code = wanted[s // CAP, s % CAP]

        def earlier(r, found):
            r = s - 1 - r
            return jnp.where(wanted[r // CAP, r % CAP] == code, r, found)

        slot = s
        if isinstance(s, int):
            for r in range(s):
                slot = earlier(r, slot)
        else:
            slot = lax.fori_loop(0, s, earlier, s)
        acc_k[slot] += back[s // CAP, s % CAP].astype(jnp.float32)
        acc_v[slot] += back[s // CAP, CAP + s % CAP].astype(jnp.float32)
        return slot

    def copies(s):
        tile, head = pair_of(wanted[s // CAP, s % CAP], head_step)
        rows = pl.ds(pl.multiple_of(tile * TILE, TILE), TILE)
        cols = pl.ds(pl.multiple_of(head * HD, HD), HD)
        return (
            pltpu.make_async_copy(out_k.at[s], dk.at[rows, cols], sems.at[0, s]),
            pltpu.make_async_copy(out_v.at[s], dv.at[rows, cols], sems.at[1, s]),
        )

    def first_of(s):
        code = wanted[s // CAP, s % CAP]

        def earlier(r, found):
            return jnp.where(wanted[r // CAP, r % CAP] == code, True, found)

        found = jnp.bool_(False)
        if isinstance(s, int):
            for r in range(s):
                found = earlier(r, found)
        else:
            found = lax.fori_loop(0, s, earlier, found)
        return jnp.logical_not(found)

    each(slots, add)
    out_k[...] = acc_k[...].astype(jnp.bfloat16)
    out_v[...] = acc_v[...].astype(jnp.bfloat16)

    def start(s):
        @pl.when(first_of(s))
        def _():
            for c in copies(s):
                c.start()

    def finish(s):
        @pl.when(first_of(s))
        def _():
            for c in copies(s):
                c.wait()

    each(slots, start)
    each(slots, finish)


def local(q_raw, k_raw, values, q_gain, k_gain, cotangent, kept_tiles):
    slab_count = lax.axis_size("slab")
    group_count = lax.axis_size("head")
    own_slab = lax.axis_index("slab")
    query_tiles, head_count, kept_count = kept_tiles.shape
    local_width = q_raw.shape[1]
    key_tiles = k_raw.shape[0] // TILE
    query_tokens, key_tokens = q_raw.shape[0], k_raw.shape[0]
    full_width = local_width * group_count
    head_step = pl.next_power_of_2(head_count)
    slots = slab_count * CAP
    vmem = pltpu.CompilerParams(vmem_limit_bytes=60 << 20)

    head_ids = jnp.arange(head_count, dtype=jnp.int32)[None, :, None]
    far_global = kept_tiles[:, :, NEAR:]
    far_owner = far_global // key_tiles
    code = far_global % key_tiles * head_step + head_ids
    slab_ids = jnp.arange(slab_count, dtype=jnp.int32)
    mine = far_owner.reshape(1, -1) == slab_ids[:, None]
    flat = code.reshape(1, -1)
    low = jnp.min(jnp.where(mine, flat, 1 << 20), axis=1)
    high = jnp.max(jnp.where(mine, flat, 0), axis=1)
    low = jnp.where(low == 1 << 20, 0, low)
    lane = jnp.arange(HD, dtype=jnp.int32)[None, :]
    request = jnp.where(lane == 0, low[:, None], high[:, None])
    wanted = lax.all_to_all(request, "slab", split_axis=0, concat_axis=0, tiled=True)
    use_slot = far_owner * CAP + (code != low[far_owner]).astype(jnp.int32)
    use_slot = use_slot.reshape(query_tiles, head_count * (kept_count - NEAR))

    k_sum = jnp.sum(jnp.square(k_raw.astype(jnp.float32)), axis=1)
    q_sum = jnp.sum(jnp.square(q_raw.astype(jnp.float32)), axis=1)
    stat_rows = -(-(key_tokens + query_tokens) // (8 * HD)) * 8
    pad = stat_rows * HD - key_tokens - query_tokens
    stats = jnp.concatenate((k_sum, q_sum, jnp.zeros((pad,), jnp.float32))).reshape(stat_rows, HD)
    parts = [stats]
    for step in range(1, group_count):
        parts.append(
            lax.ppermute(
                stats, "head", [(i, (i + step) % group_count) for i in range(group_count)]
            )
        )

    outgoing = pl.pallas_call(
        functools.partial(gather_kernel, full_width, head_step, group_count),
        out_shape=jax.ShapeDtypeStruct((slab_count, 2 * CAP, TILE, HD), jnp.bfloat16),
        in_specs=[SMEM] + [VMEM] * group_count + [VMEM, ANY, ANY],
        out_specs=VMEM,
        scratch_shapes=[
            pltpu.VMEM((slots, TILE, HD), jnp.bfloat16),
            pltpu.VMEM((key_tokens, HD), jnp.float32),
            pltpu.SemaphoreType.DMA((2, slots)),
        ],
        compiler_params=vmem,
        name="gather_far",
    )(wanted, *parts, k_gain.reshape(head_count, HD), k_raw, values)
    far = lax.all_to_all(outgoing, "slab", split_axis=0, concat_axis=0, tiled=True)

    near = kept_tiles[:, :, :NEAR] - own_slab * key_tiles
    tile_ids = jnp.arange(key_tiles, dtype=jnp.int32)
    kept = jnp.any(near[:, :, :, None] == tile_ids, axis=2)
    mask = jnp.where(kept, 0.0, MASKED).astype(jnp.float32).transpose(1, 2, 0)
    mask = jnp.repeat(mask, TILE, axis=2)

    def column(tokens):
        return pl.BlockSpec((tokens, HD), lambda h, *_: (0, h))

    def whole(*shape):
        return pl.BlockSpec(shape, lambda h, *_: (0,) * len(shape))

    def each_head(*shape):
        return pl.BlockSpec((1, *shape), lambda h, *_: (h,) + (0,) * len(shape))

    def per_head(shape, dtype):
        return jax.ShapeDtypeStruct((head_count, *shape), dtype)

    def tokens_of(count):
        return jax.ShapeDtypeStruct((count, local_width), jnp.bfloat16)

    far_shape = (slab_count, 2 * CAP, TILE, HD)
    qn, kn_t, v_t, cot_t, exps, stat = pl.pallas_call(
        functools.partial(near_kernel, full_width, group_count),
        grid=(head_count,),
        in_specs=[whole(stat_rows, HD)] * group_count
        + [
            column(query_tokens),
            column(key_tokens),
            column(key_tokens),
            column(query_tokens),
            each_head(1, HD),
            each_head(1, HD),
            each_head(key_tiles, query_tokens),
        ],
        out_specs=[
            column(query_tokens),
            each_head(HD, key_tokens),
            each_head(HD, key_tokens),
            each_head(HD, query_tokens),
            each_head(key_tokens, query_tokens),
            each_head(8, query_tokens),
        ],
        out_shape=[
            tokens_of(query_tokens),
            per_head((HD, key_tokens), jnp.bfloat16),
            per_head((HD, key_tokens), jnp.bfloat16),
            per_head((HD, query_tokens), jnp.bfloat16),
            per_head((key_tokens, query_tokens), jnp.float32),
            per_head((8, query_tokens), jnp.float32),
        ],
        scratch_shapes=[pltpu.VMEM((key_tokens, HD), jnp.bfloat16)],
        compiler_params=vmem,
        name="near",
    )(
        *parts, q_raw, k_raw, values, cotangent,
        q_gain.reshape(head_count, 1, HD), k_gain.reshape(head_count, 1, HD), mask,
    )

    attn_out, probs, delta, far_ds, far_grad = pl.pallas_call(
        meet_kernel,
        grid_spec=pltpu.PrefetchScalarGridSpec(
            num_scalar_prefetch=1,
            grid=(head_count,),
            in_specs=[
                each_head(key_tokens, query_tokens),
                each_head(8, query_tokens),
                each_head(HD, key_tokens),
                each_head(HD, query_tokens),
                column(query_tokens),
                column(query_tokens),
                whole(*far_shape),
            ],
            out_specs=[
                column(query_tokens),
                each_head(key_tokens, query_tokens),
                each_head(8, query_tokens),
                each_head(2 * TILE, query_tokens),
                whole(*far_shape),
            ],
            scratch_shapes=[pltpu.VMEM((slots, TILE, HD), jnp.float32)] * 2,
        ),
        out_shape=[
            tokens_of(query_tokens),
            per_head((key_tokens, query_tokens), jnp.bfloat16),
            per_head((8, query_tokens), jnp.float32),
            per_head((2 * TILE, query_tokens), jnp.bfloat16),
            jax.ShapeDtypeStruct(far_shape, jnp.bfloat16),
        ],
        compiler_params=vmem,
        name="meet",
    )(use_slot, exps, stat, v_t, cot_t, cotangent, qn, far)

    dq_normed, dk, dv, kept_k, kept_v = pl.pallas_call(
        functools.partial(grad_kernel, head_step),
        grid_spec=pltpu.PrefetchScalarGridSpec(
            num_scalar_prefetch=2,
            grid=(head_count,),
            in_specs=[
                each_head(HD, key_tokens),
                column(query_tokens),
                column(key_tokens),
                column(query_tokens),
                each_head(key_tokens, query_tokens),
                each_head(8, query_tokens),
                each_head(2 * TILE, query_tokens),
                whole(*far_shape),
            ],
            out_specs=[
                column(query_tokens),
                column(key_tokens),
                column(key_tokens),
                whole(slots, TILE, HD),
                whole(slots, TILE, HD),
            ],
            scratch_shapes=[
                pltpu.VMEM((key_tokens, query_tokens), jnp.bfloat16),
                pltpu.VMEM((key_tokens, HD), jnp.float32),
                pltpu.VMEM((key_tokens, HD), jnp.float32),
            ],
        ),
        out_shape=[
            tokens_of(query_tokens),
            tokens_of(key_tokens),
            tokens_of(key_tokens),
            jax.ShapeDtypeStruct((slots, TILE, HD), jnp.float32),
            jax.ShapeDtypeStruct((slots, TILE, HD), jnp.float32),
        ],
        compiler_params=vmem,
        name="grad",
    )(wanted, use_slot, kn_t, qn, values, cotangent, probs, delta, far_ds, far)

    back = lax.all_to_all(far_grad, "slab", split_axis=0, concat_axis=0, tiled=True)
    dk, dv = pl.pallas_call(
        functools.partial(finish_kernel, head_step),
        out_shape=[jax.ShapeDtypeStruct((key_tokens, local_width), jnp.bfloat16)] * 2,
        in_specs=[SMEM, VMEM, VMEM, VMEM, ANY, ANY],
        out_specs=[ANY, ANY],
        scratch_shapes=[
            pltpu.VMEM((slots, TILE, HD), jnp.float32),
            pltpu.VMEM((slots, TILE, HD), jnp.float32),
            pltpu.VMEM((slots, TILE, HD), jnp.bfloat16),
            pltpu.VMEM((slots, TILE, HD), jnp.bfloat16),
            pltpu.SemaphoreType.DMA((2, slots)),
        ],
        input_output_aliases={4: 0, 5: 1},
        compiler_params=vmem,
        name="finish",
    )(wanted, back, kept_k, kept_v, dk, dv)
    return attn_out, dq_normed, dk, dv


def solution(mesh):
    tokens = P("slab", "head")
    return jax.shard_map(
        local,
        mesh=mesh,
        in_specs=(tokens, tokens, tokens, P("head"), P("head"), tokens, P("slab", "head", None)),
        out_specs=(tokens, tokens, tokens, tokens),
        check_vma=False,
    )
```

```python
import functools
import math

import jax
import jax.numpy as jnp
from jax import lax
from jax.experimental import pallas as pl
from jax.experimental.pallas import tpu as pltpu
from jax.sharding import PartitionSpec as P

TILE = 64
NEAR = 10
CAP = 2
HD = 128

NORM_EPSILON = 1e-06
MASKED = -1e30

VMEM = pl.BlockSpec(memory_space=pltpu.VMEM)
SMEM = pl.BlockSpec(memory_space=pltpu.SMEM)
HBM = pl.BlockSpec(memory_space=pltpu.HBM)
ANYWHERE = pl.BlockSpec(memory_space=pl.ANY)
LIMIT = 1 << 20
NT = (((1,), (1,)), ((), ()))
NN = (((1,), (0,)), ((), ()))
LOG2E = math.log2(math.e)


def dot(a, b, dims):
    return lax.dot_general(a, b, dims, preferred_element_type=jnp.float32)


def each(count, body):
    if count <= 16:
        for i in range(count):
            body(i)
    else:
        lax.fori_loop(0, count, lambda i, c: (body(i), c)[1], 0)


def inverse_rms(part_refs, full_width):
    total = part_refs[0][...]
    for ref in part_refs[1:]:
        total = total + ref[...]
    return lax.rsqrt(total / full_width + NORM_EPSILON).T


def pair_of(wanted, s, head_step):
    code = wanted[s // CAP, s % CAP]
    return lax.shift_right_logical(code, head_step.bit_length() - 1), code & (head_step - 1)


def gather_kernel(full_width, head_step, parts, wanted, *refs):
    part_refs, (gain, k_raw, values, out, k_buf, v_buf, k_out, scale, sems) = (
        refs[:parts],
        refs[parts:],
    )
    slots = out.shape[0] * CAP

    def source(s):
        tile, head = pair_of(wanted, s, head_step)
        return (
            pl.ds(pl.multiple_of(tile * TILE, TILE), TILE),
            pl.ds(pl.multiple_of(head * HD, HD), HD),
        )

    def k_in(s):
        return pltpu.make_async_copy(k_raw.at[source(s)], k_buf.at[s], sems.at[0, s])

    def v_in(s):
        return pltpu.make_async_copy(values.at[source(s)], v_buf.at[s], sems.at[1, s])

    def k_copy(s):
        return pltpu.make_async_copy(k_out.at[s], out.at[s // CAP, s % CAP], sems.at[2, s])

    def v_copy(s):
        return pltpu.make_async_copy(v_buf.at[s], out.at[s // CAP, CAP + s % CAP], sems.at[3, s])

    each(slots, lambda s: v_in(s).start())
    each(slots, lambda s: k_in(s).start())
    inverse = inverse_rms(part_refs, full_width)
    for j in range(scale.shape[0] // HD):
        scale[j * HD : (j + 1) * HD, :] = jnp.broadcast_to(inverse[:, j : j + 1], (HD, HD))

    def normalize(s):
        rows, cols = source(s)
        k_in(s).wait()
        k_out[s] = (k_buf[s].astype(jnp.float32) * scale[rows, :] * gain[cols][None]).astype(
            jnp.bfloat16
        )
        k_copy(s).start()

    def forward(s):
        v_in(s).wait()
        v_copy(s).start()

    each(slots, forward)
    each(slots, normalize)
    each(slots, lambda s: v_copy(s).wait())
    each(slots, lambda s: k_copy(s).wait())


def left_half():
    return lax.broadcasted_iota(jnp.int32, (2 * TILE, HD), 1) < TILE


def pick(x):
    return jnp.where(left_half(), x[: 2 * TILE], x[2 * TILE :])


def slots_of(kept, request, key_tiles, head_step, head, p):
    slots = []
    for i in (2 * p, 2 * p + 1):
        for f in range(CAP):
            tile = kept[i, head * (NEAR + CAP) + NEAR + f]
            owner = lax.div(tile, key_tiles)
            code = (tile - owner * key_tiles) * head_step + head
            slots.append(owner * CAP + jnp.where(request[owner, 0] == LIMIT - code, 0, 1))
    return slots


def far_tiles(far, slots, first=0):
    return jnp.concatenate([far[s // CAP, first + s % CAP] for s in slots], axis=0)


def halves_t(tiles):
    return jnp.concatenate((tiles[: 2 * TILE].T, tiles[2 * TILE :].T), axis=0)


def split_rows(x):
    zero = jnp.zeros((TILE, x.shape[1]), x.dtype)
    return jnp.concatenate(
        (
            jnp.concatenate((x[:TILE], zero), axis=0),
            jnp.concatenate((zero, x[TILE:]), axis=0),
        ),
        axis=1,
    )


def near_kernel(full_width, parts, *refs):
    part_refs = refs[:parts]
    (q_raw, k_raw, values, cot, q_gain, k_gain, mask,
     kn, qn, kn_t, v_t, cot_t, stat, scores) = refs[parts:]
    key_tokens = k_raw.shape[0]
    query_tokens = q_raw.shape[0]
    exponent = LOG2E / math.sqrt(HD)

    inverse = inverse_rms(part_refs, full_width)
    first = key_tokens // HD
    for j in range(query_tokens // HD):
        rows = slice(j * HD, (j + 1) * HD)
        qn[rows, :] = (
            q_raw[rows, :].astype(jnp.float32) * inverse[:, first + j : first + j + 1] * q_gain[...]
        ).astype(jnp.bfloat16)
    for j in range(key_tokens // HD):
        rows = slice(j * HD, (j + 1) * HD)
        kn[rows, :] = (
            k_raw[rows, :].astype(jnp.float32) * inverse[:, j : j + 1] * k_gain[...]
        ).astype(jnp.bfloat16)

    step = 4 * TILE
    top = None
    for c in range(0, key_tokens, step):
        block = dot(kn[c : c + step, :], qn[...], NT) * exponent
        for t in range(step // TILE):
            rows = slice(c + t * TILE, c + (t + 1) * TILE)
            tile = block[t * TILE : (t + 1) * TILE] + mask[0, c // TILE + t, :][None]
            scores[rows, :] = tile
            tile = jnp.max(tile.reshape(TILE // 8, 8, query_tokens), axis=0)
            top = tile if top is None else jnp.maximum(top, tile)
    top = jnp.max(top, axis=0, keepdims=True)
    total = jnp.zeros((8, query_tokens), jnp.float32)
    for c in range(0, key_tokens, TILE):
        e = jnp.exp2(scores[c : c + TILE, :] - top)
        total = total + jnp.sum(e.reshape(TILE // 8, 8, query_tokens), axis=0)
    stat[0, 0:1, :] = top
    stat[0, 1:2, :] = jnp.sum(total, axis=0, keepdims=True)
    kn_t[0] = kn[...].T
    v_t[0] = values[...].T
    cot_t[0] = cot[...].T


def meet_kernel(head_step, kept, request, kn_in, qn_in, stat_in, mask_in, v_t_in, cot_t_in, cot_in,
                far_in, attn_out, probs_out, delta_out, far_ds_out, far_k_out, far_grad_out,
                far, kn, qn, stat, mask, v_t, cot_t, cot, attn, probs, delta, far_ds, far_p, outs,
                logs, k_acc, v_acc, far_grad, in_sems, out_sems):
    heads, key_tiles, query_tokens = mask.shape
    pairs = query_tokens // HD
    score_scale = 1.0 / math.sqrt(HD)
    exponent = score_scale * LOG2E
    slots = far.shape[0] * CAP

    def lanes(h):
        return slice(h * HD, (h + 1) * HD)

    fetches = [
        [
            pltpu.make_async_copy(src, dst, in_sems.at[h, n])
            for n, (src, dst) in enumerate(
                (
                    (qn_in.at[:, lanes(h)], qn.at[:, lanes(h)]),
                    (stat_in.at[h], stat.at[h]),
                    (mask_in.at[h], mask.at[h]),
                    (kn_in.at[:, lanes(h)], kn.at[:, lanes(h)]),
                    (v_t_in.at[h], v_t.at[h]),
                    (cot_t_in.at[h], cot_t.at[h]),
                    (cot_in.at[:, lanes(h)], cot.at[:, lanes(h)]),
                )
            )
        ]
        for h in range(heads)
    ]
    fetch_far = pltpu.make_async_copy(far_in, far, in_sems.at[heads, 0])
    fetch_far.start()
    for first, last in ((0, 2), (2, 5), (5, 7)):
        for h in range(heads):
            for copy in fetches[h][first:last]:
                copy.start()
    stores = []
    k_acc[...] = jnp.zeros_like(k_acc)
    v_acc[...] = jnp.zeros_like(v_acc)
    used = [
        [slots_of(kept, request, key_tiles, head_step, h, p) for p in range(pairs)]
        for h in range(heads)
    ]

    def far_scores(h):
        for copy in fetches[h][:2]:
            copy.wait()
        for p in range(pairs):
            cols = slice(p * HD, (p + 1) * HD)
            far_s = pick(dot(far_tiles(far, used[h][p]), qn[cols, lanes(h)], NT)) * exponent
            near_top = stat[h, 0:1, cols]
            top = jnp.maximum(near_top, jnp.max(far_s, axis=0, keepdims=True))
            total = stat[h, 1:2, cols] * jnp.exp2(near_top - top) + jnp.sum(
                jnp.exp2(far_s - top), axis=0, keepdims=True
            )
            log_total = top + jnp.log2(total)
            logs[h, 0:1, cols] = log_total
            far_p[h, :, cols] = jnp.exp2(far_s - log_total).astype(jnp.bfloat16)

    step = 4 * TILE

    def near_part(h):
        for copy in fetches[h][2:5]:
            copy.wait()
        for c in range(0, key_tiles * TILE, step):
            block = dot(kn[c : c + step, lanes(h)], qn[:, lanes(h)], NT) * exponent
            for t in range(step // TILE):
                row = mask[h, c // TILE + t, :][None] - logs[h, 0:1, :]
                probs[h, c + t * TILE : c + (t + 1) * TILE, :] = jnp.exp2(
                    block[t * TILE : (t + 1) * TILE] + row
                ).astype(jnp.bfloat16)
        outs[h] = dot(v_t[h], probs[h], NN)
        stores.append(pltpu.make_async_copy(probs.at[h], probs_out.at[h], out_sems.at[h]))
        stores[-1].start()

    def far_part(h):
        for copy in fetches[h][5:]:
            copy.wait()
        for p in range(pairs):
            cols = slice(p * HD, (p + 1) * HD)
            values = far_tiles(far, used[h][p], CAP)
            weights = far_p[h, :, cols]
            out_b = (outs[h, :, cols] + pick(dot(halves_t(values), weights, NN))).astype(
                jnp.bfloat16
            )
            attn[cols, lanes(h)] = out_b.T
            row_delta = jnp.sum(
                cot_t[h, :, cols].astype(jnp.float32) * out_b.astype(jnp.float32),
                axis=0, keepdims=True,
            )
            delta[h, 0:1, cols] = row_delta
            grad_p = pick(dot(values, cot[cols, lanes(h)], NT))
            ds = (weights.astype(jnp.float32) * (grad_p - row_delta) * score_scale).astype(
                jnp.bfloat16
            )
            far_ds[h, :, cols] = ds
            grad_k = dot(ds, split_rows(qn[cols, lanes(h)]), NN)
            grad_v = dot(weights, split_rows(cot[cols, lanes(h)]), NN)
            for n, s in enumerate(used[h][p]):
                rows = slice(n % CAP * TILE, (n % CAP + 1) * TILE)
                half = slice(n // CAP * HD, (n // CAP + 1) * HD)
                k_acc[s] += grad_k[rows, half]
                v_acc[s] += grad_v[rows, half]

    fetch_far.wait()
    stores.append(pltpu.make_async_copy(far.at[:, :CAP], far_k_out, out_sems.at[heads]))
    stores[-1].start()
    for h in range(heads):
        far_scores(h)
    near_part(0)
    for h in range(1, heads):
        near_part(h)
        far_part(h - 1)
    far_part(heads - 1)

    def send(s):
        far_grad[s // CAP, s % CAP] = k_acc[s].astype(jnp.bfloat16)
        far_grad[s // CAP, CAP + s % CAP] = v_acc[s].astype(jnp.bfloat16)

    each(slots, send)
    for n, (src, dst) in enumerate(
        ((far_grad, far_grad_out), (attn, attn_out), (delta, delta_out), (far_ds, far_ds_out))
    ):
        stores.append(pltpu.make_async_copy(src, dst, out_sems.at[heads + 1 + n]))
        stores[-1].start()
    for copy in stores:
        copy.wait()


def grad_kernel(head_step, kept, request, wanted, kn_t_in, qn_in, values_in, cot_in, probs_in,
                delta_in, far_ds_in, far_k_in, dq_out, dk_out, dv_out, tiles_out,
                kn_t, qn, values, cot, pair, delta, far_ds, far_k, weights, acc,
                dq, dk, dv, in_sems, out_sems, tile_sems):
    heads, key_tokens = pair.shape[:2]
    query_tokens = qn.shape[0]
    score_scale = 1.0 / math.sqrt(HD)
    slots = far_k.shape[0] * CAP
    step = 4 * TILE

    def lanes(h):
        return slice(h * HD, (h + 1) * HD)

    fetches = [
        [
            pltpu.make_async_copy(src, dst, in_sems.at[h, n])
            for n, (src, dst) in enumerate(
                (
                    (values_in.at[:, lanes(h)], values.at[:, lanes(h)]),
                    (cot_in.at[:, lanes(h)], cot.at[:, lanes(h)]),
                    (probs_in.at[h], pair.at[h, :, query_tokens:]),
                    (delta_in.at[h], delta.at[h]),
                    (qn_in.at[:, lanes(h)], qn.at[:, lanes(h)]),
                    (kn_t_in.at[h], kn_t.at[h]),
                    (far_ds_in.at[h], far_ds.at[h]),
                )
            )
        ]
        for h in range(heads)
    ]
    far_fetch = pltpu.make_async_copy(far_k_in, far_k, in_sems.at[heads, 0])
    for first, last in ((0, 5), (5, 7)):
        for h in range(heads):
            for copy in fetches[h][first:last]:
                copy.start()
    far_fetch.start()
    weights[...] = jnp.zeros_like(weights)
    stores = []
    for h in range(heads):
        for copy in fetches[h][:5]:
            copy.wait()
        weights[h % 2, :query_tokens, :HD] = qn[:, lanes(h)]
        weights[h % 2, query_tokens:, HD:] = cot[:, lanes(h)]
        for c in range(0, key_tokens, step):
            rows = slice(c, c + step)
            dp = dot(values[rows, lanes(h)], cot[:, lanes(h)], NT)
            pair[h, rows, :query_tokens] = (
                pair[h, rows, query_tokens:].astype(jnp.float32)
                * (dp - delta[h, 0:1, :])
                * score_scale
            ).astype(jnp.bfloat16)
        for c in range(0, key_tokens, step):
            rows = slice(c, c + step)
            both = dot(pair[h, rows, :], weights[h % 2], NN)
            acc[h, rows, :] = both
            dk[rows, lanes(h)] = both[:, :HD].astype(jnp.bfloat16)
            dv[rows, lanes(h)] = both[:, HD:].astype(jnp.bfloat16)
        for n, (src, dst) in enumerate(((dk, dk_out), (dv, dv_out))):
            stores.append(
                pltpu.make_async_copy(
                    src.at[:, lanes(h)], dst.at[:, lanes(h)], out_sems.at[h, n]
                )
            )
            stores[-1].start()

    def keep(s):
        tile, owner = pair_of(wanted, s, head_step)
        rows = pl.ds(pl.multiple_of(tile * TILE, TILE), TILE)
        return pltpu.make_async_copy(acc.at[owner, rows, :], tiles_out.at[s], tile_sems.at[s])

    each(slots, lambda s: keep(s).start())
    far_fetch.wait()
    for h in range(heads):
        for copy in fetches[h][5:]:
            copy.wait()
        dq_t = dot(kn_t[h], pair[h, :, :query_tokens], NN)
        for p in range(query_tokens // HD):
            cols = slice(p * HD, (p + 1) * HD)
            used = slots_of(kept, request, key_tokens // TILE, head_step, h, p)
            far_part = pick(dot(halves_t(far_tiles(far_k, used)), far_ds[h, :, cols], NN))
            dq[cols, lanes(h)] = (dq_t[:, cols] + far_part).astype(jnp.bfloat16).T
    stores.append(pltpu.make_async_copy(dq, dq_out, out_sems.at[heads, 0]))
    stores[-1].start()
    each(slots, lambda s: keep(s).wait())
    for copy in stores:
        copy.wait()


def finish_kernel(head_step, wanted, back_in, tiles, dk_in, dv_in, dk, dv, back, acc, out_k, out_v, sems):
    del dk_in, dv_in
    slots = back.shape[0] * CAP
    fetches = [
        pltpu.make_async_copy(back_in, back, sems.at[2, 0]),
        pltpu.make_async_copy(tiles, acc, sems.at[2, 1]),
    ]
    for fetch in fetches:
        fetch.start()

    def code_of(s):
        return wanted[s // CAP, s % CAP]

    def first_slot(s):
        code = code_of(s)
        if isinstance(s, int):
            found = jnp.int32(s)
            for r in reversed(range(s)):
                found = jnp.where(codes[r] == code, r, found)
            return found
        return lax.fori_loop(
            0, s, lambda r, f: jnp.where(code_of(s - 1 - r) == code, s - 1 - r, f), s
        )

    codes = [code_of(s) for s in range(slots)] if slots <= 16 else None

    def copies(s):
        tile, head = pair_of(wanted, s, head_step)
        rows = pl.ds(pl.multiple_of(tile * TILE, TILE), TILE)
        cols = pl.ds(pl.multiple_of(head * HD, HD), HD)
        return (
            pltpu.make_async_copy(out_k.at[s], dk.at[rows, cols], sems.at[0, s]),
            pltpu.make_async_copy(out_v.at[s], dv.at[rows, cols], sems.at[1, s]),
        )

    def add(s):
        slot = firsts[s] if firsts else first_slot(s)
        acc[slot, :, :HD] += back[s // CAP, s % CAP].astype(jnp.float32)
        acc[slot, :, HD:] += back[s // CAP, CAP + s % CAP].astype(jnp.float32)

    def start(s):
        @pl.when((firsts[s] if firsts else first_slot(s)) == s)
        def _():
            out_k[s] = acc[s, :, :HD].astype(jnp.bfloat16)
            out_v[s] = acc[s, :, HD:].astype(jnp.bfloat16)
            for c in copies(s):
                c.start()

    def finish(s):
        @pl.when((firsts[s] if firsts else first_slot(s)) == s)
        def _():
            for c in copies(s):
                c.wait()

    firsts = [first_slot(s) for s in range(slots)] if slots <= 16 else None
    for fetch in fetches:
        fetch.wait()
    each(slots, add)
    each(slots, start)
    each(slots, finish)


def local(q_raw, k_raw, values, q_gain, k_gain, cotangent, kept_tiles):
    slab_count = lax.axis_size("slab")
    group_count = lax.axis_size("head")
    own_slab = lax.axis_index("slab")
    query_tiles, head_count, kept_count = kept_tiles.shape
    local_width = q_raw.shape[1]
    key_tiles = k_raw.shape[0] // TILE
    query_tokens, key_tokens = q_raw.shape[0], k_raw.shape[0]
    full_width = local_width * group_count
    head_step = pl.next_power_of_2(head_count)
    slots = slab_count * CAP
    vmem = pltpu.CompilerParams(vmem_limit_bytes=60 << 20)

    def grant(limit):
        return pltpu.CompilerParams(vmem_limit_bytes=limit)


    def array(shape, dtype=jnp.bfloat16):
        return jax.ShapeDtypeStruct(shape, dtype)

    by_head = kept_tiles.transpose(1, 0, 2)
    owner = lax.div(by_head, key_tiles)
    code = (by_head - owner * key_tiles) * head_step + lax.broadcasted_iota(
        jnp.int32, by_head.shape, 0
    )
    owner = jnp.where(lax.broadcasted_iota(jnp.int32, by_head.shape, 2) < NEAR, -1, owner)
    mine = owner[None] == jnp.arange(slab_count, dtype=jnp.int32)[:, None, None, None]
    low = jnp.max(jnp.where(mine, LIMIT - code[None], 0), axis=(1, 2, 3))
    high = jnp.max(jnp.where(mine, code[None] + 1, 0), axis=(1, 2, 3))
    lane = jnp.arange(HD, dtype=jnp.int32)[None, :]
    request = jnp.where(lane == 0, low[:, None], high[:, None])
    wanted = lax.all_to_all(
        jnp.broadcast_to(request[:, None], (slab_count, 8, HD)),
        "slab", split_axis=0, concat_axis=0, tiled=True,
    )[:, 0]
    wanted = jnp.where(wanted == 0, 0, jnp.where(lane == 0, LIMIT - wanted, wanted - 1))
    kept_flat = kept_tiles.reshape(query_tiles, head_count * kept_count)

    key_rows, query_rows = key_tokens // HD, query_tokens // HD
    stat_rows = -(-(key_rows + query_rows) // 8) * 8
    k_sum = jnp.sum(jnp.square(k_raw.astype(jnp.float32)), axis=1)
    q_sum = jnp.sum(jnp.square(q_raw.astype(jnp.float32)), axis=1)
    pad = (stat_rows - key_rows - query_rows) * HD
    stats = jnp.concatenate((k_sum, q_sum, jnp.zeros((pad,), jnp.float32))).reshape(stat_rows, HD)
    parts = [stats]
    for step in range(1, group_count):
        parts.append(
            lax.ppermute(
                stats, "head", [(i, (i + step) % group_count) for i in range(group_count)]
            )
        )

    q_row, k_row = q_gain.reshape(1, local_width), k_gain.reshape(1, local_width)
    far_shape = (slab_count, 2 * CAP, TILE, HD)
    outgoing = pl.pallas_call(
        functools.partial(gather_kernel, full_width, head_step, group_count),
        out_shape=array(far_shape),
        in_specs=[SMEM] + [VMEM] * group_count + [VMEM, HBM, HBM],
        out_specs=HBM,
        scratch_shapes=[
            pltpu.VMEM((slots, TILE, HD), jnp.bfloat16),
            pltpu.VMEM((slots, TILE, HD), jnp.bfloat16),
            pltpu.VMEM((slots, TILE, HD), jnp.bfloat16),
            pltpu.VMEM((key_tokens, HD), jnp.float32),
            pltpu.SemaphoreType.DMA((4, slots)),
        ],
        compiler_params=grant(62700000),
        name="gather_far",
    )(wanted, *parts, k_gain, k_raw, values)
    far = lax.all_to_all(outgoing, "slab", split_axis=0, concat_axis=0, tiled=True)

    near = kept_tiles[:, :, :NEAR] - own_slab * key_tiles
    tile_ids = jnp.arange(key_tiles, dtype=jnp.int32)
    kept = jnp.any(near[:, :, :, None] == tile_ids, axis=2)
    mask = jnp.where(kept, 0.0, MASKED).astype(jnp.float32).transpose(1, 2, 0)
    mask = jnp.repeat(mask, TILE, axis=2)

    def column(tokens):
        return pl.BlockSpec((tokens, HD), lambda h: (0, h))

    def each_head(*shape):
        return pl.BlockSpec((1, *shape), lambda h: (h,) + (0,) * len(shape))

    all_stats = pl.BlockSpec((stat_rows, HD), lambda h: (0, 0))
    gain_spec = pl.BlockSpec((1, HD), lambda h: (0, h))
    queries, keys = (query_tokens, local_width), (key_tokens, local_width)
    keys_t, queries_t = (head_count, HD, key_tokens), (head_count, HD, query_tokens)
    stat_shape = (head_count, 8, query_tokens)
    probs_shape = (head_count, key_tokens, query_tokens)
    far_ds_shape = (head_count, 2 * TILE, query_tokens)
    far_k_shape = (slab_count, CAP, TILE, HD)
    kn, qn, kn_t, v_t, cot_t, stat = pl.pallas_call(
        functools.partial(near_kernel, full_width, group_count),
        grid=(head_count,),
        in_specs=[all_stats] * group_count
        + [
            column(query_tokens),
            column(key_tokens),
            column(key_tokens),
            column(query_tokens),
            gain_spec,
            gain_spec,
            each_head(key_tiles, query_tokens),
        ],
        out_specs=[
            column(key_tokens),
            column(query_tokens),
            each_head(HD, key_tokens),
            each_head(HD, key_tokens),
            each_head(HD, query_tokens),
            each_head(8, query_tokens),
        ],
        out_shape=[
            array(keys),
            array(queries),
            array(keys_t),
            array(keys_t),
            array(queries_t),
            array(stat_shape, jnp.float32),
        ],
        scratch_shapes=[pltpu.VMEM((key_tokens, query_tokens), jnp.float32)],
        compiler_params=pltpu.CompilerParams(vmem_limit_bytes=60 << 20),
        name="near",
    )(*parts, q_raw, k_raw, values, cotangent, q_row, k_row, mask)

    attn_out, probs, delta, far_ds, far_k, far_grad = pl.pallas_call(
        functools.partial(meet_kernel, head_step),
        in_specs=[SMEM] * 2 + [HBM] * 8,
        out_specs=[HBM] * 6,
        out_shape=[
            array(queries),
            array(probs_shape),
            array(stat_shape, jnp.float32),
            array(far_ds_shape),
            array(far_k_shape),
            array(far_shape),
        ],
        scratch_shapes=[
            pltpu.VMEM(far_shape, jnp.bfloat16),
            pltpu.VMEM(keys, jnp.bfloat16),
            pltpu.VMEM(queries, jnp.bfloat16),
            pltpu.VMEM(stat_shape, jnp.float32),
            pltpu.VMEM((head_count, key_tiles, query_tokens), jnp.float32),
            pltpu.VMEM(keys_t, jnp.bfloat16),
            pltpu.VMEM(queries_t, jnp.bfloat16),
            pltpu.VMEM(queries, jnp.bfloat16),
            pltpu.VMEM(queries, jnp.bfloat16),
            pltpu.VMEM(probs_shape, jnp.bfloat16),
            pltpu.VMEM(stat_shape, jnp.float32),
            pltpu.VMEM(far_ds_shape, jnp.bfloat16),
            pltpu.VMEM(far_ds_shape, jnp.bfloat16),
            pltpu.VMEM(queries_t, jnp.float32),
            pltpu.VMEM(stat_shape, jnp.float32),
            pltpu.VMEM((slots, TILE, HD), jnp.float32),
            pltpu.VMEM((slots, TILE, HD), jnp.float32),
            pltpu.VMEM(far_shape, jnp.bfloat16),
            pltpu.SemaphoreType.DMA((head_count + 1, 7)),
            pltpu.SemaphoreType.DMA((head_count + 5,)),
        ],
        compiler_params=vmem,
        name="meet",
    )(kept_flat, request, kn, qn, stat, mask, v_t, cot_t, cotangent, far)
    back = lax.all_to_all(far_grad, "slab", split_axis=0, concat_axis=0, tiled=True)

    dq_normed, dk, dv, tiles = pl.pallas_call(
        functools.partial(grad_kernel, head_step),
        in_specs=[SMEM] * 3 + [HBM] * 8,
        out_specs=[HBM] * 4,
        out_shape=[
            array(queries),
            array(keys),
            array(keys),
            array((slots, TILE, 2 * HD), jnp.float32),
        ],
        scratch_shapes=[
            pltpu.VMEM(keys_t, jnp.bfloat16),
            pltpu.VMEM(queries, jnp.bfloat16),
            pltpu.VMEM(keys, jnp.bfloat16),
            pltpu.VMEM(queries, jnp.bfloat16),
            pltpu.VMEM((head_count, key_tokens, 2 * query_tokens), jnp.bfloat16),
            pltpu.VMEM(stat_shape, jnp.float32),
            pltpu.VMEM(far_ds_shape, jnp.bfloat16),
            pltpu.VMEM(far_k_shape, jnp.bfloat16),
            pltpu.VMEM((2, 2 * query_tokens, 2 * HD), jnp.bfloat16),
            pltpu.VMEM((head_count, key_tokens, 2 * HD), jnp.float32),
            pltpu.VMEM(queries, jnp.bfloat16),
            pltpu.VMEM(keys, jnp.bfloat16),
            pltpu.VMEM(keys, jnp.bfloat16),
            pltpu.SemaphoreType.DMA((head_count + 1, 7)),
            pltpu.SemaphoreType.DMA((head_count + 1, 2)),
            pltpu.SemaphoreType.DMA((slots,)),
        ],
        compiler_params=vmem,
        name="grad",
    )(kept_flat, request, wanted, kn_t, qn, values, cotangent, probs, delta, far_ds, far_k)

    dk, dv = pl.pallas_call(
        functools.partial(finish_kernel, head_step),
        out_shape=[array(keys), array(keys)],
        in_specs=[SMEM, ANYWHERE, HBM, HBM, HBM],
        out_specs=[HBM, HBM],
        scratch_shapes=[
            pltpu.VMEM(far_shape, jnp.bfloat16),
            pltpu.VMEM((slots, TILE, 2 * HD), jnp.float32),
            pltpu.VMEM((slots, TILE, HD), jnp.bfloat16),
            pltpu.VMEM((slots, TILE, HD), jnp.bfloat16),
            pltpu.SemaphoreType.DMA((3, slots)),
        ],
        input_output_aliases={3: 0, 4: 1},
        compiler_params=grant(50 << 20),
        name="finish",
    )(wanted, back, tiles, dk, dv)
    return attn_out, dq_normed, dk, dv


def solution(mesh):
    tokens = P("slab", "head")
    return jax.shard_map(
        local,
        mesh=mesh,
        in_specs=(tokens, tokens, tokens, P("head"), P("head"), tokens, P("slab", "head", None)),
        out_specs=(tokens, tokens, tokens, tokens),
        check_vma=False,
    )
```

```python
import functools
import math

import jax
import jax.numpy as jnp
from jax import lax
from jax.experimental import pallas as pl
from jax.experimental.pallas import tpu as pltpu
from jax.sharding import PartitionSpec as P

TILE = 64
NEAR = 10
CAP = 2
HD = 128

NORM_EPSILON = 1e-06
MASKED = -1e30

VMEM = pl.BlockSpec(memory_space=pltpu.VMEM)
SMEM = pl.BlockSpec(memory_space=pltpu.SMEM)
HBM = pl.BlockSpec(memory_space=pltpu.HBM)
ANYWHERE = pl.BlockSpec(memory_space=pl.ANY)
LIMIT = 1 << 20
NT = (((1,), (1,)), ((), ()))
NN = (((1,), (0,)), ((), ()))
LOG2E = math.log2(math.e)


def dot(a, b, dims):
    return lax.dot_general(a, b, dims, preferred_element_type=jnp.float32)


def each(count, body):
    if count <= 16:
        for i in range(count):
            body(i)
    else:
        lax.fori_loop(0, count, lambda i, c: (body(i), c)[1], 0)


def inverse_rms(part_refs, full_width):
    total = part_refs[0][...]
    for ref in part_refs[1:]:
        total = total + ref[...]
    return lax.rsqrt(total / full_width + NORM_EPSILON).T


def pair_of(wanted, s, head_step):
    code = wanted[s // CAP, s % CAP]
    return lax.shift_right_logical(code, head_step.bit_length() - 1), code & (head_step - 1)


def gather_kernel(full_width, head_step, parts, wanted, *refs):
    part_refs, (gain, k_raw, values, out, k_buf, v_buf, k_out, scale, sems) = (
        refs[:parts],
        refs[parts:],
    )
    slots = out.shape[0] * CAP

    def source(s):
        tile, head = pair_of(wanted, s, head_step)
        return (
            pl.ds(pl.multiple_of(tile * TILE, TILE), TILE),
            pl.ds(pl.multiple_of(head * HD, HD), HD),
        )

    def k_in(s):
        return pltpu.make_async_copy(k_raw.at[source(s)], k_buf.at[s], sems.at[0, s])

    def v_in(s):
        return pltpu.make_async_copy(values.at[source(s)], v_buf.at[s], sems.at[1, s])

    def k_copy(s):
        return pltpu.make_async_copy(k_out.at[s], out.at[s // CAP, s % CAP], sems.at[2, s])

    def v_copy(s):
        return pltpu.make_async_copy(v_buf.at[s], out.at[s // CAP, CAP + s % CAP], sems.at[3, s])

    each(slots, lambda s: v_in(s).start())
    each(slots, lambda s: k_in(s).start())
    inverse = inverse_rms(part_refs, full_width)
    for j in range(scale.shape[0] // HD):
        scale[j * HD : (j + 1) * HD, :] = jnp.broadcast_to(inverse[:, j : j + 1], (HD, HD))

    def normalize(s):
        rows, cols = source(s)
        k_in(s).wait()
        k_out[s] = (k_buf[s].astype(jnp.float32) * scale[rows, :] * gain[cols][None]).astype(
            jnp.bfloat16
        )
        k_copy(s).start()

    def forward(s):
        v_in(s).wait()
        v_copy(s).start()

    each(slots, forward)
    each(slots, normalize)
    each(slots, lambda s: v_copy(s).wait())
    each(slots, lambda s: k_copy(s).wait())


def left_half():
    return lax.broadcasted_iota(jnp.int32, (2 * TILE, HD), 1) < TILE


def pick(x):
    return jnp.where(left_half(), x[: 2 * TILE], x[2 * TILE :])


def slots_of(kept, request, key_tiles, head_step, head, p):
    slots = []
    for i in (2 * p, 2 * p + 1):
        for f in range(CAP):
            tile = kept[i, head * (NEAR + CAP) + NEAR + f]
            owner = lax.div(tile, key_tiles)
            code = (tile - owner * key_tiles) * head_step + head
            slots.append(owner * CAP + jnp.where(request[owner, 0] == LIMIT - code, 0, 1))
    return slots


def far_tiles(far, slots, first=0):
    return jnp.concatenate([far[s // CAP, first + s % CAP] for s in slots], axis=0)


def halves_t(tiles):
    return jnp.concatenate((tiles[: 2 * TILE].T, tiles[2 * TILE :].T), axis=0)


def split_rows(x):
    zero = jnp.zeros((TILE, x.shape[1]), x.dtype)
    return jnp.concatenate(
        (
            jnp.concatenate((x[:TILE], zero), axis=0),
            jnp.concatenate((zero, x[TILE:]), axis=0),
        ),
        axis=1,
    )


def near_kernel(full_width, parts, *refs):
    part_refs = refs[:parts]
    (q_raw, k_raw, values, cot, q_gain, k_gain, mask,
     kn, qn, kn_t, v_t, cot_t, stat, scores) = refs[parts:]
    key_tokens = k_raw.shape[0]
    query_tokens = q_raw.shape[0]
    exponent = LOG2E / math.sqrt(HD)

    inverse = inverse_rms(part_refs, full_width)
    first = key_tokens // HD
    for j in range(query_tokens // HD):
        rows = slice(j * HD, (j + 1) * HD)
        qn[rows, :] = (
            q_raw[rows, :].astype(jnp.float32) * inverse[:, first + j : first + j + 1] * q_gain[...]
        ).astype(jnp.bfloat16)
    for j in range(key_tokens // HD):
        rows = slice(j * HD, (j + 1) * HD)
        kn[rows, :] = (
            k_raw[rows, :].astype(jnp.float32) * inverse[:, j : j + 1] * k_gain[...]
        ).astype(jnp.bfloat16)

    step = 4 * TILE
    top = None
    for c in range(0, key_tokens, step):
        block = dot(kn[c : c + step, :], qn[...], NT) * exponent
        for t in range(step // TILE):
            rows = slice(c + t * TILE, c + (t + 1) * TILE)
            tile = block[t * TILE : (t + 1) * TILE] + mask[0, c // TILE + t, :][None]
            scores[rows, :] = tile
            tile = jnp.max(tile.reshape(TILE // 8, 8, query_tokens), axis=0)
            top = tile if top is None else jnp.maximum(top, tile)
    top = jnp.max(top, axis=0, keepdims=True)
    total = jnp.zeros((8, query_tokens), jnp.float32)
    for c in range(0, key_tokens, TILE):
        e = jnp.exp2(scores[c : c + TILE, :] - top)
        total = total + jnp.sum(e.reshape(TILE // 8, 8, query_tokens), axis=0)
    stat[0, 0:1, :] = top
    stat[0, 1:2, :] = jnp.sum(total, axis=0, keepdims=True)
    kn_t[0] = kn[...].T
    v_t[0] = values[...].T
    cot_t[0] = cot[...].T


def loop(count, body):
    lax.fori_loop(0, count, lambda i, carry: (body(i), carry)[1], 0)


def lanes(h):
    return pl.ds(pl.multiple_of(h * HD, HD), HD)


def meet_kernel(head_step, kept, request, kn_in, qn_in, stat_in, mask_in, v_t_in, cot_t_in, cot_in,
                far_in, attn_out, probs_out, delta_out, far_ds_out, far_k_out, far_grad_out,
                far, kn, qn, stat, mask, v_t, cot_t, cot, attn, probs, delta, far_ds, far_p, outs,
                logs, k_acc, v_acc, far_grad, in_sems, out_sems):
    heads, key_tiles, query_tokens = mask.shape
    pairs = query_tokens // HD
    score_scale = 1.0 / math.sqrt(HD)
    exponent = score_scale * LOG2E
    slots = far.shape[0] * CAP

    def fetches(h):
        return [
            pltpu.make_async_copy(src, dst, in_sems.at[h, n])
            for n, (src, dst) in enumerate(
                (
                    (qn_in.at[:, lanes(h)], qn.at[h]),
                    (stat_in.at[h], stat.at[h]),
                    (mask_in.at[h], mask.at[h]),
                    (kn_in.at[:, lanes(h)], kn.at[h]),
                    (v_t_in.at[h], v_t.at[h]),
                    (cot_t_in.at[h], cot_t.at[h]),
                    (cot_in.at[:, lanes(h)], cot.at[h]),
                )
            )
        ]

    fetch_far = pltpu.make_async_copy(far_in, far, in_sems.at[heads, 0])
    far_store = pltpu.make_async_copy(far.at[:, :CAP], far_k_out, out_sems.at[heads, 0])

    def head_stores(h):
        return (
            pltpu.make_async_copy(probs.at[h], probs_out.at[h], out_sems.at[h, 0]),
            pltpu.make_async_copy(attn.at[h], attn_out.at[:, lanes(h)], out_sems.at[h, 1]),
        )

    fetch_far.start()
    loop(heads, lambda h: [copy.start() for copy in fetches(h)[:2]])
    loop(heads, lambda h: [copy.start() for copy in fetches(h)[2:]])
    k_acc[...] = jnp.zeros_like(k_acc)
    v_acc[...] = jnp.zeros_like(v_acc)
    fetch_far.wait()
    far_store.start()

    def used(h, p):
        return slots_of(kept, request, key_tiles, head_step, h, p)

    def far_scores(h):
        for copy in fetches(h)[:2]:
            copy.wait()
        for p in range(pairs):
            cols = slice(p * HD, (p + 1) * HD)
            far_s = pick(dot(far_tiles(far, used(h, p)), qn[h, cols, :], NT)) * exponent
            near_top = stat[h, 0:1, cols]
            top = jnp.maximum(near_top, jnp.max(far_s, axis=0, keepdims=True))
            total = stat[h, 1:2, cols] * jnp.exp2(near_top - top) + jnp.sum(
                jnp.exp2(far_s - top), axis=0, keepdims=True
            )
            log_total = top + jnp.log2(total)
            logs[h, 0:1, cols] = log_total
            far_p[h, :, cols] = jnp.exp2(far_s - log_total).astype(jnp.bfloat16)

    step = 4 * TILE

    def near_part(h):
        for copy in fetches(h)[2:]:
            copy.wait()

        for first in range(0, key_tiles * TILE, step):
            block = dot(kn[h, first : first + step, :], qn[h], NT) * exponent
            for t in range(step // TILE):
                row = mask[h, first // TILE + t, :][None] - logs[h, 0:1, :]
                probs[h, first + t * TILE : first + (t + 1) * TILE, :] = jnp.exp2(
                    block[t * TILE : (t + 1) * TILE] + row
                ).astype(jnp.bfloat16)

        head_stores(h)[0].start()
        outs[...] = dot(v_t[h], probs[h], NN)
        for p in range(pairs):
            cols = slice(p * HD, (p + 1) * HD)
            slot = used(h, p)
            values = far_tiles(far, slot, CAP)
            weights = far_p[h, :, cols]
            out_b = (outs[:, cols] + pick(dot(halves_t(values), weights, NN))).astype(
                jnp.bfloat16
            )
            attn[h, cols, :] = out_b.T
            row_delta = jnp.sum(
                cot_t[h, :, cols].astype(jnp.float32) * out_b.astype(jnp.float32),
                axis=0, keepdims=True,
            )
            delta[h, 0:1, cols] = row_delta
            grad_p = pick(dot(values, cot[h, cols, :], NT))
            ds = (weights.astype(jnp.float32) * (grad_p - row_delta) * score_scale).astype(
                jnp.bfloat16
            )
            far_ds[h, :, cols] = ds
            grad_k = dot(ds, split_rows(qn[h, cols, :]), NN)
            grad_v = dot(weights, split_rows(cot[h, cols, :]), NN)
            for n, s in enumerate(slot):
                rows = slice(n % CAP * TILE, (n % CAP + 1) * TILE)
                half = slice(n // CAP * HD, (n // CAP + 1) * HD)
                k_acc[s] += grad_k[rows, half]
                v_acc[s] += grad_v[rows, half]
        head_stores(h)[1].start()

    each(heads, far_scores)
    loop(heads, near_part)

    def send(s):
        far_grad[s // CAP, s % CAP] = k_acc[s].astype(jnp.bfloat16)
        far_grad[s // CAP, CAP + s % CAP] = v_acc[s].astype(jnp.bfloat16)

    each(slots, send)
    stores = [
        pltpu.make_async_copy(src, dst, out_sems.at[heads, 1 + n])
        for n, (src, dst) in enumerate(
            ((far_grad, far_grad_out), (delta, delta_out), (far_ds, far_ds_out))
        )
    ]
    for copy in stores:
        copy.start()
    loop(heads, lambda h: [copy.wait() for copy in head_stores(h)])
    for copy in [far_store, *stores]:
        copy.wait()


def grad_kernel(head_step, kept, request, wanted, kn_t_in, qn_in, values_in, cot_in, probs_in,
                delta_in, far_ds_in, far_k_in, dq_out, dk_out, dv_out, tiles_out,
                kn_t, qn, values, cot, pair, delta, far_ds, far_k, weights, acc,
                dq, dk, dv, in_sems, out_sems, tile_sems):
    heads, key_tokens = pair.shape[:2]
    query_tokens = qn.shape[0]
    score_scale = 1.0 / math.sqrt(HD)
    slots = far_k.shape[0] * CAP
    step = 4 * TILE

    def lanes(h):
        return slice(h * HD, (h + 1) * HD)

    fetches = [
        [
            pltpu.make_async_copy(src, dst, in_sems.at[h, n])
            for n, (src, dst) in enumerate(
                (
                    (values_in.at[:, lanes(h)], values.at[:, lanes(h)]),
                    (cot_in.at[:, lanes(h)], cot.at[:, lanes(h)]),
                    (probs_in.at[h], pair.at[h, :, query_tokens:]),
                    (delta_in.at[h], delta.at[h]),
                    (qn_in.at[:, lanes(h)], qn.at[:, lanes(h)]),
                    (kn_t_in.at[h], kn_t.at[h]),
                    (far_ds_in.at[h], far_ds.at[h]),
                )
            )
        ]
        for h in range(heads)
    ]
    far_fetch = pltpu.make_async_copy(far_k_in, far_k, in_sems.at[heads, 0])
    for first, last in ((0, 5), (5, 7)):
        for h in range(heads):
            for copy in fetches[h][first:last]:
                copy.start()
    far_fetch.start()
    weights[...] = jnp.zeros_like(weights)
    stores = []
    for h in range(heads):
        for copy in fetches[h][:5]:
            copy.wait()
        weights[h % 2, :query_tokens, :HD] = qn[:, lanes(h)]
        weights[h % 2, query_tokens:, HD:] = cot[:, lanes(h)]
        for c in range(0, key_tokens, step):
            rows = slice(c, c + step)
            dp = dot(values[rows, lanes(h)], cot[:, lanes(h)], NT)
            pair[h, rows, :query_tokens] = (
                pair[h, rows, query_tokens:].astype(jnp.float32)
                * (dp - delta[h, 0:1, :])
                * score_scale
            ).astype(jnp.bfloat16)
        for c in range(0, key_tokens, step):
            rows = slice(c, c + step)
            both = dot(pair[h, rows, :], weights[h % 2], NN)
            acc[h, rows, :] = both
            dk[rows, lanes(h)] = both[:, :HD].astype(jnp.bfloat16)
            dv[rows, lanes(h)] = both[:, HD:].astype(jnp.bfloat16)
        for n, (src, dst) in enumerate(((dk, dk_out), (dv, dv_out))):
            stores.append(
                pltpu.make_async_copy(
                    src.at[:, lanes(h)], dst.at[:, lanes(h)], out_sems.at[h, n]
                )
            )
            stores[-1].start()

    def keep(s):
        tile, owner = pair_of(wanted, s, head_step)
        rows = pl.ds(pl.multiple_of(tile * TILE, TILE), TILE)
        return pltpu.make_async_copy(acc.at[owner, rows, :], tiles_out.at[s], tile_sems.at[s])

    each(slots, lambda s: keep(s).start())
    far_fetch.wait()
    for h in range(heads):
        for copy in fetches[h][5:]:
            copy.wait()
        dq_t = dot(kn_t[h], pair[h, :, :query_tokens], NN)
        for p in range(query_tokens // HD):
            cols = slice(p * HD, (p + 1) * HD)
            used = slots_of(kept, request, key_tokens // TILE, head_step, h, p)
            far_part = pick(dot(halves_t(far_tiles(far_k, used)), far_ds[h, :, cols], NN))
            dq[cols, lanes(h)] = (dq_t[:, cols] + far_part).astype(jnp.bfloat16).T
    stores.append(pltpu.make_async_copy(dq, dq_out, out_sems.at[heads, 0]))
    stores[-1].start()
    each(slots, lambda s: keep(s).wait())
    for copy in stores:
        copy.wait()


def finish_kernel(head_step, wanted, back_in, tiles, dk_in, dv_in, dk, dv, back, acc, out_k, out_v, sems):
    del dk_in, dv_in
    slots = back.shape[0] * CAP
    fetches = [
        pltpu.make_async_copy(back_in, back, sems.at[2, 0]),
        pltpu.make_async_copy(tiles, acc, sems.at[2, 1]),
    ]
    for fetch in fetches:
        fetch.start()

    def code_of(s):
        return wanted[s // CAP, s % CAP]

    def first_slot(s):
        code = code_of(s)
        if isinstance(s, int):
            found = jnp.int32(s)
            for r in reversed(range(s)):
                found = jnp.where(codes[r] == code, r, found)
            return found
        return lax.fori_loop(
            0, s, lambda r, f: jnp.where(code_of(s - 1 - r) == code, s - 1 - r, f), s
        )

    codes = [code_of(s) for s in range(slots)] if slots <= 16 else None

    def copies(s):
        tile, head = pair_of(wanted, s, head_step)
        rows = pl.ds(pl.multiple_of(tile * TILE, TILE), TILE)
        cols = pl.ds(pl.multiple_of(head * HD, HD), HD)
        return (
            pltpu.make_async_copy(out_k.at[s], dk.at[rows, cols], sems.at[0, s]),
            pltpu.make_async_copy(out_v.at[s], dv.at[rows, cols], sems.at[1, s]),
        )

    def add(s):
        slot = firsts[s] if firsts else first_slot(s)
        acc[slot, :, :HD] += back[s // CAP, s % CAP].astype(jnp.float32)
        acc[slot, :, HD:] += back[s // CAP, CAP + s % CAP].astype(jnp.float32)

    def start(s):
        @pl.when((firsts[s] if firsts else first_slot(s)) == s)
        def _():
            out_k[s] = acc[s, :, :HD].astype(jnp.bfloat16)
            out_v[s] = acc[s, :, HD:].astype(jnp.bfloat16)
            for c in copies(s):
                c.start()

    def finish(s):
        @pl.when((firsts[s] if firsts else first_slot(s)) == s)
        def _():
            for c in copies(s):
                c.wait()

    firsts = [first_slot(s) for s in range(slots)] if slots <= 16 else None
    for fetch in fetches:
        fetch.wait()
    each(slots, add)
    each(slots, start)
    each(slots, finish)


def local(q_raw, k_raw, values, q_gain, k_gain, cotangent, kept_tiles):
    slab_count = lax.axis_size("slab")
    group_count = lax.axis_size("head")
    own_slab = lax.axis_index("slab")
    query_tiles, head_count, kept_count = kept_tiles.shape
    local_width = q_raw.shape[1]
    key_tiles = k_raw.shape[0] // TILE
    query_tokens, key_tokens = q_raw.shape[0], k_raw.shape[0]
    full_width = local_width * group_count
    head_step = pl.next_power_of_2(head_count)
    slots = slab_count * CAP
    vmem = pltpu.CompilerParams(vmem_limit_bytes=60 << 20)

    def grant(limit):
        return pltpu.CompilerParams(vmem_limit_bytes=limit)


    def array(shape, dtype=jnp.bfloat16):
        return jax.ShapeDtypeStruct(shape, dtype)

    by_head = kept_tiles.transpose(1, 0, 2)
    owner = lax.div(by_head, key_tiles)
    code = (by_head - owner * key_tiles) * head_step + lax.broadcasted_iota(
        jnp.int32, by_head.shape, 0
    )
    owner = jnp.where(lax.broadcasted_iota(jnp.int32, by_head.shape, 2) < NEAR, -1, owner)
    mine = owner[None] == jnp.arange(slab_count, dtype=jnp.int32)[:, None, None, None]
    low = jnp.max(jnp.where(mine, LIMIT - code[None], 0), axis=(1, 2, 3))
    high = jnp.max(jnp.where(mine, code[None] + 1, 0), axis=(1, 2, 3))
    lane = jnp.arange(HD, dtype=jnp.int32)[None, :]
    request = jnp.where(lane == 0, low[:, None], high[:, None])
    wanted = lax.all_to_all(
        jnp.broadcast_to(request[:, None], (slab_count, 8, HD)),
        "slab", split_axis=0, concat_axis=0, tiled=True,
    )[:, 0]
    wanted = jnp.where(wanted == 0, 0, jnp.where(lane == 0, LIMIT - wanted, wanted - 1))
    kept_flat = kept_tiles.reshape(query_tiles, head_count * kept_count)

    key_rows, query_rows = key_tokens // HD, query_tokens // HD
    stat_rows = -(-(key_rows + query_rows) // 8) * 8
    k_sum = jnp.sum(jnp.square(k_raw.astype(jnp.float32)), axis=1)
    q_sum = jnp.sum(jnp.square(q_raw.astype(jnp.float32)), axis=1)
    pad = (stat_rows - key_rows - query_rows) * HD
    stats = jnp.concatenate((k_sum, q_sum, jnp.zeros((pad,), jnp.float32))).reshape(stat_rows, HD)
    parts = [stats]
    for step in range(1, group_count):
        parts.append(
            lax.ppermute(
                stats, "head", [(i, (i + step) % group_count) for i in range(group_count)]
            )
        )

    q_row, k_row = q_gain.reshape(1, local_width), k_gain.reshape(1, local_width)
    far_shape = (slab_count, 2 * CAP, TILE, HD)
    outgoing = pl.pallas_call(
        functools.partial(gather_kernel, full_width, head_step, group_count),
        out_shape=array(far_shape),
        in_specs=[SMEM] + [VMEM] * group_count + [VMEM, HBM, HBM],
        out_specs=HBM,
        scratch_shapes=[
            pltpu.VMEM((slots, TILE, HD), jnp.bfloat16),
            pltpu.VMEM((slots, TILE, HD), jnp.bfloat16),
            pltpu.VMEM((slots, TILE, HD), jnp.bfloat16),
            pltpu.VMEM((key_tokens, HD), jnp.float32),
            pltpu.SemaphoreType.DMA((4, slots)),
        ],
        compiler_params=grant(62700000),
        name="gather_far",
    )(wanted, *parts, k_gain, k_raw, values)
    far = lax.all_to_all(outgoing, "slab", split_axis=0, concat_axis=0, tiled=True)

    near = kept_tiles[:, :, :NEAR] - own_slab * key_tiles
    tile_ids = jnp.arange(key_tiles, dtype=jnp.int32)
    kept = jnp.any(near[:, :, :, None] == tile_ids, axis=2)
    mask = jnp.where(kept, 0.0, MASKED).astype(jnp.float32).transpose(1, 2, 0)
    mask = jnp.repeat(mask, TILE, axis=2)

    def column(tokens):
        return pl.BlockSpec((tokens, HD), lambda h: (0, h))

    def each_head(*shape):
        return pl.BlockSpec((1, *shape), lambda h: (h,) + (0,) * len(shape))

    all_stats = pl.BlockSpec((stat_rows, HD), lambda h: (0, 0))
    gain_spec = pl.BlockSpec((1, HD), lambda h: (0, h))
    queries, keys = (query_tokens, local_width), (key_tokens, local_width)
    keys_h, queries_h = (head_count, key_tokens, HD), (head_count, query_tokens, HD)
    keys_t, queries_t = (head_count, HD, key_tokens), (head_count, HD, query_tokens)
    stat_shape = (head_count, 8, query_tokens)
    probs_shape = (head_count, key_tokens, query_tokens)
    far_ds_shape = (head_count, 2 * TILE, query_tokens)
    far_k_shape = (slab_count, CAP, TILE, HD)
    kn, qn, kn_t, v_t, cot_t, stat = pl.pallas_call(
        functools.partial(near_kernel, full_width, group_count),
        grid=(head_count,),
        in_specs=[all_stats] * group_count
        + [
            column(query_tokens),
            column(key_tokens),
            column(key_tokens),
            column(query_tokens),
            gain_spec,
            gain_spec,
            each_head(key_tiles, query_tokens),
        ],
        out_specs=[
            column(key_tokens),
            column(query_tokens),
            each_head(HD, key_tokens),
            each_head(HD, key_tokens),
            each_head(HD, query_tokens),
            each_head(8, query_tokens),
        ],
        out_shape=[
            array(keys),
            array(queries),
            array(keys_t),
            array(keys_t),
            array(queries_t),
            array(stat_shape, jnp.float32),
        ],
        scratch_shapes=[pltpu.VMEM((key_tokens, query_tokens), jnp.float32)],
        compiler_params=pltpu.CompilerParams(vmem_limit_bytes=60 << 20),
        name="near",
    )(*parts, q_raw, k_raw, values, cotangent, q_row, k_row, mask)

    attn_out, probs, delta, far_ds, far_k, far_grad = pl.pallas_call(
        functools.partial(meet_kernel, head_step),
        in_specs=[SMEM] * 2 + [HBM] * 8,
        out_specs=[HBM] * 6,
        out_shape=[
            array(queries),
            array(probs_shape),
            array(stat_shape, jnp.float32),
            array(far_ds_shape),
            array(far_k_shape),
            array(far_shape),
        ],
        scratch_shapes=[
            pltpu.VMEM(far_shape, jnp.bfloat16),
            pltpu.VMEM(keys_h, jnp.bfloat16),
            pltpu.VMEM(queries_h, jnp.bfloat16),
            pltpu.VMEM(stat_shape, jnp.float32),
            pltpu.VMEM((head_count, key_tiles, query_tokens), jnp.float32),
            pltpu.VMEM(keys_t, jnp.bfloat16),
            pltpu.VMEM(queries_t, jnp.bfloat16),
            pltpu.VMEM(queries_h, jnp.bfloat16),
            pltpu.VMEM(queries_h, jnp.bfloat16),
            pltpu.VMEM(probs_shape, jnp.bfloat16),
            pltpu.VMEM(stat_shape, jnp.float32),
            pltpu.VMEM(far_ds_shape, jnp.bfloat16),
            pltpu.VMEM(far_ds_shape, jnp.bfloat16),
            pltpu.VMEM((HD, query_tokens), jnp.float32),
            pltpu.VMEM(stat_shape, jnp.float32),
            pltpu.VMEM((slots, TILE, HD), jnp.float32),
            pltpu.VMEM((slots, TILE, HD), jnp.float32),
            pltpu.VMEM(far_shape, jnp.bfloat16),
            pltpu.SemaphoreType.DMA((head_count + 1, 7)),
            pltpu.SemaphoreType.DMA((head_count + 1, 4)),
        ],
        compiler_params=vmem,
        name="meet",
    )(kept_flat, request, kn, qn, stat, mask, v_t, cot_t, cotangent, far)
    back = lax.all_to_all(far_grad, "slab", split_axis=0, concat_axis=0, tiled=True)

    dq_normed, dk, dv, tiles = pl.pallas_call(
        functools.partial(grad_kernel, head_step),
        in_specs=[SMEM] * 3 + [HBM] * 8,
        out_specs=[HBM] * 4,
        out_shape=[
            array(queries),
            array(keys),
            array(keys),
            array((slots, TILE, 2 * HD), jnp.float32),
        ],
        scratch_shapes=[
            pltpu.VMEM(keys_t, jnp.bfloat16),
            pltpu.VMEM(queries, jnp.bfloat16),
            pltpu.VMEM(keys, jnp.bfloat16),
            pltpu.VMEM(queries, jnp.bfloat16),
            pltpu.VMEM((head_count, key_tokens, 2 * query_tokens), jnp.bfloat16),
            pltpu.VMEM(stat_shape, jnp.float32),
            pltpu.VMEM(far_ds_shape, jnp.bfloat16),
            pltpu.VMEM(far_k_shape, jnp.bfloat16),
            pltpu.VMEM((2, 2 * query_tokens, 2 * HD), jnp.bfloat16),
            pltpu.VMEM((head_count, key_tokens, 2 * HD), jnp.float32),
            pltpu.VMEM(queries, jnp.bfloat16),
            pltpu.VMEM(keys, jnp.bfloat16),
            pltpu.VMEM(keys, jnp.bfloat16),
            pltpu.SemaphoreType.DMA((head_count + 1, 7)),
            pltpu.SemaphoreType.DMA((head_count + 1, 2)),
            pltpu.SemaphoreType.DMA((slots,)),
        ],
        compiler_params=vmem,
        name="grad",
    )(kept_flat, request, wanted, kn_t, qn, values, cotangent, probs, delta, far_ds, far_k)

    dk, dv = pl.pallas_call(
        functools.partial(finish_kernel, head_step),
        out_shape=[array(keys), array(keys)],
        in_specs=[SMEM, ANYWHERE, HBM, HBM, HBM],
        out_specs=[HBM, HBM],
        scratch_shapes=[
            pltpu.VMEM(far_shape, jnp.bfloat16),
            pltpu.VMEM((slots, TILE, 2 * HD), jnp.float32),
            pltpu.VMEM((slots, TILE, HD), jnp.bfloat16),
            pltpu.VMEM((slots, TILE, HD), jnp.bfloat16),
            pltpu.SemaphoreType.DMA((3, slots)),
        ],
        input_output_aliases={3: 0, 4: 1},
        compiler_params=grant(50 << 20),
        name="finish",
    )(wanted, back, tiles, dk, dv)
    return attn_out, dq_normed, dk, dv


def solution(mesh):
    tokens = P("slab", "head")
    return jax.shard_map(
        local,
        mesh=mesh,
        in_specs=(tokens, tokens, tokens, P("head"), P("head"), tokens, P("slab", "head", None)),
        out_specs=(tokens, tokens, tokens, tokens),
        check_vma=False,
    )
```

```python
import functools
import math

import jax
import jax.numpy as jnp
from jax import lax
from jax.experimental import pallas as pl
from jax.experimental.pallas import tpu as pltpu
from jax.sharding import PartitionSpec as P

TILE = 64
NEAR = 10
CAP = 2
HD = 128

NORM_EPSILON = 1e-06
MASKED = -1e30

VMEM = pl.BlockSpec(memory_space=pltpu.VMEM)
SMEM = pl.BlockSpec(memory_space=pltpu.SMEM)
HBM = pl.BlockSpec(memory_space=pltpu.HBM)
ANYWHERE = pl.BlockSpec(memory_space=pl.ANY)
LIMIT = 1 << 20
NT = (((1,), (1,)), ((), ()))
NN = (((1,), (0,)), ((), ()))
LOG2E = math.log2(math.e)


def dot(a, b, dims):
    return lax.dot_general(a, b, dims, preferred_element_type=jnp.float32)


def each(count, body):
    if count <= 16:
        for i in range(count):
            body(i)
    else:
        lax.fori_loop(0, count, lambda i, c: (body(i), c)[1], 0)


def inverse_rms(part_refs, full_width):
    total = part_refs[0][...]
    for ref in part_refs[1:]:
        total = total + ref[...]
    return lax.rsqrt(total / full_width + NORM_EPSILON).T


def pair_of(wanted, s, head_step):
    code = wanted[s // CAP, s % CAP]
    return lax.shift_right_logical(code, head_step.bit_length() - 1), code & (head_step - 1)


def gather_kernel(full_width, head_step, parts, wanted, *refs):
    part_refs, (gain, k_raw, values, out, k_buf, v_buf, k_out, scale, sems) = (
        refs[:parts],
        refs[parts:],
    )
    slots = out.shape[0] * CAP

    def source(s):
        tile, head = pair_of(wanted, s, head_step)
        return (
            pl.ds(pl.multiple_of(tile * TILE, TILE), TILE),
            pl.ds(pl.multiple_of(head * HD, HD), HD),
        )

    def k_in(s):
        return pltpu.make_async_copy(k_raw.at[source(s)], k_buf.at[s], sems.at[0, s])

    def v_in(s):
        return pltpu.make_async_copy(values.at[source(s)], v_buf.at[s], sems.at[1, s])

    def k_copy(s):
        return pltpu.make_async_copy(k_out.at[s], out.at[s // CAP, s % CAP], sems.at[2, s])

    def v_copy(s):
        return pltpu.make_async_copy(v_buf.at[s], out.at[s // CAP, CAP + s % CAP], sems.at[3, s])

    each(slots, lambda s: v_in(s).start())
    each(slots, lambda s: k_in(s).start())
    inverse = inverse_rms(part_refs, full_width)
    for j in range(scale.shape[0] // HD):
        scale[j * HD : (j + 1) * HD, :] = jnp.broadcast_to(inverse[:, j : j + 1], (HD, HD))

    def normalize(s):
        rows, cols = source(s)
        k_in(s).wait()
        k_out[s] = (k_buf[s].astype(jnp.float32) * scale[rows, :] * gain[cols][None]).astype(
            jnp.bfloat16
        )
        k_copy(s).start()

    def forward(s):
        v_in(s).wait()
        v_copy(s).start()

    each(slots, forward)
    each(slots, normalize)
    each(slots, lambda s: v_copy(s).wait())
    each(slots, lambda s: k_copy(s).wait())


def left_half():
    return lax.broadcasted_iota(jnp.int32, (2 * TILE, HD), 1) < TILE


def pick(x):
    return jnp.where(left_half(), x[: 2 * TILE], x[2 * TILE :])


def slots_of(kept, request, key_tiles, head_step, head, p):
    slots = []
    for i in (2 * p, 2 * p + 1):
        for f in range(CAP):
            tile = kept[i, head * (NEAR + CAP) + NEAR + f]
            owner = lax.div(tile, key_tiles)
            code = (tile - owner * key_tiles) * head_step + head
            slots.append(owner * CAP + jnp.where(request[owner, 0] == LIMIT - code, 0, 1))
    return slots


def far_tiles(far, slots, first=0):
    return jnp.concatenate([far[s // CAP, first + s % CAP] for s in slots], axis=0)


def halves_t(tiles):
    return jnp.concatenate((tiles[: 2 * TILE].T, tiles[2 * TILE :].T), axis=0)


def split_rows(x):
    zero = jnp.zeros((TILE, x.shape[1]), x.dtype)
    return jnp.concatenate(
        (
            jnp.concatenate((x[:TILE], zero), axis=0),
            jnp.concatenate((zero, x[TILE:]), axis=0),
        ),
        axis=1,
    )


def near_kernel(full_width, parts, *refs):
    part_refs = refs[:parts]
    (q_raw, k_raw, values, cot, q_gain, k_gain, mask,
     kn, qn, kn_t, v_t, cot_t, stat, scores) = refs[parts:]
    key_tokens = k_raw.shape[0]
    query_tokens = q_raw.shape[0]
    exponent = LOG2E / math.sqrt(HD)

    inverse = inverse_rms(part_refs, full_width)
    first = key_tokens // HD
    for j in range(query_tokens // HD):
        rows = slice(j * HD, (j + 1) * HD)
        qn[rows, :] = (
            q_raw[rows, :].astype(jnp.float32) * inverse[:, first + j : first + j + 1] * q_gain[...]
        ).astype(jnp.bfloat16)
    for j in range(key_tokens // HD):
        rows = slice(j * HD, (j + 1) * HD)
        kn[rows, :] = (
            k_raw[rows, :].astype(jnp.float32) * inverse[:, j : j + 1] * k_gain[...]
        ).astype(jnp.bfloat16)

    step = 4 * TILE
    top = None
    for c in range(0, key_tokens, step):
        block = dot(kn[c : c + step, :], qn[...], NT) * exponent
        for t in range(step // TILE):
            rows = slice(c + t * TILE, c + (t + 1) * TILE)
            tile = block[t * TILE : (t + 1) * TILE] + mask[0, c // TILE + t, :][None]
            scores[rows, :] = tile
            tile = jnp.max(tile.reshape(TILE // 8, 8, query_tokens), axis=0)
            top = tile if top is None else jnp.maximum(top, tile)
    top = jnp.max(top, axis=0, keepdims=True)
    total = jnp.zeros((8, query_tokens), jnp.float32)
    for c in range(0, key_tokens, TILE):
        e = jnp.exp2(scores[c : c + TILE, :] - top)
        total = total + jnp.sum(e.reshape(TILE // 8, 8, query_tokens), axis=0)
    stat[0, 0:1, :] = top
    stat[0, 1:2, :] = jnp.sum(total, axis=0, keepdims=True)
    kn_t[0] = kn[...].T
    v_t[0] = values[...].T
    cot_t[0] = cot[...].T


def loop(count, body):
    lax.fori_loop(0, count, lambda i, carry: (body(i), carry)[1], 0)


def lanes(h):
    return pl.ds(pl.multiple_of(h * HD, HD), HD)


def meet_kernel(head_step, kept, request, kn_in, qn_in, stat_in, mask_in, v_t_in, cot_t_in, cot_in,
                far_in, attn_out, probs_out, delta_out, far_ds_out, far_k_out, far_grad_out,
                far, kn, qn, stat, mask, v_t, cot_t, cot, attn, probs, delta, far_ds, far_p, outs,
                logs, k_acc, v_acc, far_grad, in_sems, out_sems):
    heads, key_tiles, query_tokens = mask.shape
    pairs = query_tokens // HD
    score_scale = 1.0 / math.sqrt(HD)
    exponent = score_scale * LOG2E
    slots = far.shape[0] * CAP

    def fetches(h):
        return [
            pltpu.make_async_copy(src, dst, in_sems.at[h, n])
            for n, (src, dst) in enumerate(
                (
                    (qn_in.at[:, lanes(h)], qn.at[h]),
                    (stat_in.at[h], stat.at[h]),
                    (mask_in.at[h], mask.at[h]),
                    (kn_in.at[:, lanes(h)], kn.at[h]),
                    (v_t_in.at[h], v_t.at[h]),
                    (cot_t_in.at[h], cot_t.at[h]),
                    (cot_in.at[:, lanes(h)], cot.at[h]),
                )
            )
        ]

    fetch_far = pltpu.make_async_copy(far_in, far, in_sems.at[heads, 0])
    far_store = pltpu.make_async_copy(far.at[:, :CAP], far_k_out, out_sems.at[heads, 0])

    def head_stores(h):
        return (
            pltpu.make_async_copy(probs.at[h], probs_out.at[h], out_sems.at[h, 0]),
            pltpu.make_async_copy(attn.at[h], attn_out.at[:, lanes(h)], out_sems.at[h, 1]),
        )

    fetch_far.start()
    loop(heads, lambda h: [copy.start() for copy in fetches(h)[:2]])
    loop(heads, lambda h: [copy.start() for copy in fetches(h)[2:]])
    k_acc[...] = jnp.zeros_like(k_acc)
    v_acc[...] = jnp.zeros_like(v_acc)
    fetch_far.wait()
    far_store.start()

    def used(h, p):
        return slots_of(kept, request, key_tiles, head_step, h, p)

    def far_scores(h):
        for copy in fetches(h)[:2]:
            copy.wait()
        for p in range(pairs):
            cols = slice(p * HD, (p + 1) * HD)
            far_s = pick(dot(far_tiles(far, used(h, p)), qn[h, cols, :], NT)) * exponent
            near_top = stat[h, 0:1, cols]
            top = jnp.maximum(near_top, jnp.max(far_s, axis=0, keepdims=True))
            total = stat[h, 1:2, cols] * jnp.exp2(near_top - top) + jnp.sum(
                jnp.exp2(far_s - top), axis=0, keepdims=True
            )
            log_total = top + jnp.log2(total)
            logs[h, 0:1, cols] = log_total
            far_p[h, :, cols] = jnp.exp2(far_s - log_total).astype(jnp.bfloat16)

    step = 4 * TILE

    def near_part(h):
        for copy in fetches(h)[2:]:
            copy.wait()

        for first in range(0, key_tiles * TILE, step):
            block = dot(kn[h, first : first + step, :], qn[h], NT) * exponent
            for t in range(step // TILE):
                row = mask[h, first // TILE + t, :][None] - logs[h, 0:1, :]
                probs[h, first + t * TILE : first + (t + 1) * TILE, :] = jnp.exp2(
                    block[t * TILE : (t + 1) * TILE] + row
                ).astype(jnp.bfloat16)

        head_stores(h)[0].start()
        outs[...] = dot(v_t[h], probs[h], NN)
        for p in range(pairs):
            cols = slice(p * HD, (p + 1) * HD)
            slot = used(h, p)
            values = far_tiles(far, slot, CAP)
            weights = far_p[h, :, cols]
            out_b = (outs[:, cols] + pick(dot(halves_t(values), weights, NN))).astype(
                jnp.bfloat16
            )
            attn[h, cols, :] = out_b.T
            row_delta = jnp.sum(
                cot_t[h, :, cols].astype(jnp.float32) * out_b.astype(jnp.float32),
                axis=0, keepdims=True,
            )
            delta[h, 0:1, cols] = row_delta
            grad_p = pick(dot(values, cot[h, cols, :], NT))
            ds = (weights.astype(jnp.float32) * (grad_p - row_delta) * score_scale).astype(
                jnp.bfloat16
            )
            far_ds[h, :, cols] = ds
            grad_k = dot(ds, split_rows(qn[h, cols, :]), NN)
            grad_v = dot(weights, split_rows(cot[h, cols, :]), NN)
            for n, s in enumerate(slot):
                rows = slice(n % CAP * TILE, (n % CAP + 1) * TILE)
                half = slice(n // CAP * HD, (n // CAP + 1) * HD)
                k_acc[s] += grad_k[rows, half]
                v_acc[s] += grad_v[rows, half]
        head_stores(h)[1].start()

    each(heads, far_scores)
    loop(heads, near_part)

    def send(s):
        far_grad[s // CAP, s % CAP] = k_acc[s].astype(jnp.bfloat16)
        far_grad[s // CAP, CAP + s % CAP] = v_acc[s].astype(jnp.bfloat16)

    each(slots, send)
    stores = [
        pltpu.make_async_copy(src, dst, out_sems.at[heads, 1 + n])
        for n, (src, dst) in enumerate(
            ((far_grad, far_grad_out), (delta, delta_out), (far_ds, far_ds_out))
        )
    ]
    for copy in stores:
        copy.start()
    loop(heads, lambda h: [copy.wait() for copy in head_stores(h)])
    for copy in [far_store, *stores]:
        copy.wait()


def grad_kernel(head_step, kept, request, wanted, kn_t_in, qn_in, values_in, cot_in, probs_in,
                delta_in, far_ds_in, far_k_in, dq_out, dk_out, dv_out, tiles_out,
                kn_t, qn, values, cot, pair, delta, far_ds, far_k, weights, acc,
                dq, dk, dv, in_sems, out_sems, tile_sems):
    heads, key_tokens = pair.shape[:2]
    query_tokens = qn.shape[0]
    score_scale = 1.0 / math.sqrt(HD)
    slots = far_k.shape[0] * CAP
    step = 4 * TILE

    def lanes(h):
        return slice(h * HD, (h + 1) * HD)

    fetches = [
        [
            pltpu.make_async_copy(src, dst, in_sems.at[h, n])
            for n, (src, dst) in enumerate(
                (
                    (values_in.at[:, lanes(h)], values.at[:, lanes(h)]),
                    (cot_in.at[:, lanes(h)], cot.at[:, lanes(h)]),
                    (probs_in.at[h], pair.at[h, :, query_tokens:]),
                    (delta_in.at[h], delta.at[h]),
                    (qn_in.at[:, lanes(h)], qn.at[:, lanes(h)]),
                    (kn_t_in.at[h], kn_t.at[h]),
                    (far_ds_in.at[h], far_ds.at[h]),
                )
            )
        ]
        for h in range(heads)
    ]
    far_fetch = pltpu.make_async_copy(far_k_in, far_k, in_sems.at[heads, 0])
    for first, last in ((0, 5), (5, 7)):
        for h in range(heads):
            for copy in fetches[h][first:last]:
                copy.start()
    far_fetch.start()
    weights[...] = jnp.zeros_like(weights)
    stores = []
    for h in range(heads):
        for copy in fetches[h][:5]:
            copy.wait()
        weights[h % 2, :query_tokens, :HD] = qn[:, lanes(h)]
        weights[h % 2, query_tokens:, HD:] = cot[:, lanes(h)]
        for c in range(0, key_tokens, step):
            rows = slice(c, c + step)
            dp = dot(values[rows, lanes(h)], cot[:, lanes(h)], NT)
            pair[h, rows, :query_tokens] = (
                pair[h, rows, query_tokens:].astype(jnp.float32)
                * (dp - delta[h, 0:1, :])
                * score_scale
            ).astype(jnp.bfloat16)
        for c in range(0, key_tokens, step):
            rows = slice(c, c + step)
            both = dot(pair[h, rows, :], weights[h % 2], NN)
            acc[h, rows, :] = both
            dk[rows, lanes(h)] = both[:, :HD].astype(jnp.bfloat16)
            dv[rows, lanes(h)] = both[:, HD:].astype(jnp.bfloat16)
        for n, (src, dst) in enumerate(((dk, dk_out), (dv, dv_out))):
            stores.append(
                pltpu.make_async_copy(
                    src.at[:, lanes(h)], dst.at[:, lanes(h)], out_sems.at[h, n]
                )
            )
            stores[-1].start()

    def keep(s):
        tile, owner = pair_of(wanted, s, head_step)
        rows = pl.ds(pl.multiple_of(tile * TILE, TILE), TILE)
        return pltpu.make_async_copy(acc.at[owner, rows, :], tiles_out.at[s], tile_sems.at[s])

    each(slots, lambda s: keep(s).start())
    far_fetch.wait()
    for h in range(heads):
        for copy in fetches[h][5:]:
            copy.wait()
        dq_t = dot(kn_t[h], pair[h, :, :query_tokens], NN)
        for p in range(query_tokens // HD):
            cols = slice(p * HD, (p + 1) * HD)
            used = slots_of(kept, request, key_tokens // TILE, head_step, h, p)
            far_part = pick(dot(halves_t(far_tiles(far_k, used)), far_ds[h, :, cols], NN))
            dq[cols, lanes(h)] = (dq_t[:, cols] + far_part).astype(jnp.bfloat16).T
    stores.append(pltpu.make_async_copy(dq, dq_out, out_sems.at[heads, 0]))
    stores[-1].start()
    each(slots, lambda s: keep(s).wait())
    for copy in stores:
        copy.wait()


def finish_kernel(head_step, wanted, back_in, tiles, dk_in, dv_in, dk, dv, back, acc, out_k, out_v, sems):
    del dk_in, dv_in
    slots = back.shape[0] * CAP
    fetches = [
        pltpu.make_async_copy(back_in, back, sems.at[2, 0]),
        pltpu.make_async_copy(tiles, acc, sems.at[2, 1]),
    ]
    for fetch in fetches:
        fetch.start()

    def code_of(s):
        return wanted[s // CAP, s % CAP]

    def first_slot(s):
        code = code_of(s)
        if isinstance(s, int):
            found = jnp.int32(s)
            for r in reversed(range(s)):
                found = jnp.where(codes[r] == code, r, found)
            return found
        return lax.fori_loop(
            0, s, lambda r, f: jnp.where(code_of(s - 1 - r) == code, s - 1 - r, f), s
        )

    codes = [code_of(s) for s in range(slots)] if slots <= 16 else None

    def copies(s):
        tile, head = pair_of(wanted, s, head_step)
        rows = pl.ds(pl.multiple_of(tile * TILE, TILE), TILE)
        cols = pl.ds(pl.multiple_of(head * HD, HD), HD)
        return (
            pltpu.make_async_copy(out_k.at[s], dk.at[rows, cols], sems.at[0, s]),
            pltpu.make_async_copy(out_v.at[s], dv.at[rows, cols], sems.at[1, s]),
        )

    def add(s):
        slot = firsts[s] if firsts else first_slot(s)
        acc[slot, :, :HD] += back[s // CAP, s % CAP].astype(jnp.float32)
        acc[slot, :, HD:] += back[s // CAP, CAP + s % CAP].astype(jnp.float32)

    def start(s):
        @pl.when((firsts[s] if firsts else first_slot(s)) == s)
        def _():
            out_k[s] = acc[s, :, :HD].astype(jnp.bfloat16)
            out_v[s] = acc[s, :, HD:].astype(jnp.bfloat16)
            for c in copies(s):
                c.start()

    def finish(s):
        @pl.when((firsts[s] if firsts else first_slot(s)) == s)
        def _():
            for c in copies(s):
                c.wait()

    firsts = [first_slot(s) for s in range(slots)] if slots <= 16 else None
    for fetch in fetches:
        fetch.wait()
    each(slots, add)
    each(slots, start)
    each(slots, finish)


def local(q_raw, k_raw, values, q_gain, k_gain, cotangent, kept_tiles):
    slab_count = lax.axis_size("slab")
    group_count = lax.axis_size("head")
    own_slab = lax.axis_index("slab")
    query_tiles, head_count, kept_count = kept_tiles.shape
    local_width = q_raw.shape[1]
    key_tiles = k_raw.shape[0] // TILE
    query_tokens, key_tokens = q_raw.shape[0], k_raw.shape[0]
    full_width = local_width * group_count
    head_step = pl.next_power_of_2(head_count)
    slots = slab_count * CAP
    vmem = pltpu.CompilerParams(vmem_limit_bytes=60 << 20)

    def grant(limit):
        return pltpu.CompilerParams(vmem_limit_bytes=limit)


    def array(shape, dtype=jnp.bfloat16):
        return jax.ShapeDtypeStruct(shape, dtype)

    by_head = kept_tiles.transpose(1, 0, 2)
    owner = lax.div(by_head, key_tiles)
    code = (by_head - owner * key_tiles) * head_step + lax.broadcasted_iota(
        jnp.int32, by_head.shape, 0
    )
    owner = jnp.where(lax.broadcasted_iota(jnp.int32, by_head.shape, 2) < NEAR, -1, owner)
    mine = owner[None] == jnp.arange(slab_count, dtype=jnp.int32)[:, None, None, None]
    low = jnp.max(jnp.where(mine, LIMIT - code[None], 0), axis=(1, 2, 3))
    high = jnp.max(jnp.where(mine, code[None] + 1, 0), axis=(1, 2, 3))
    lane = jnp.arange(HD, dtype=jnp.int32)[None, :]
    request = jnp.where(lane == 0, low[:, None], high[:, None])
    wanted = lax.all_to_all(
        jnp.broadcast_to(request[:, None], (slab_count, 4, HD)),
        "slab", split_axis=0, concat_axis=0, tiled=True,
    )[:, 0]
    wanted = jnp.where(wanted == 0, 0, jnp.where(lane == 0, LIMIT - wanted, wanted - 1))
    kept_flat = kept_tiles.reshape(query_tiles, head_count * kept_count)

    key_rows, query_rows = key_tokens // HD, query_tokens // HD
    stat_rows = -(-(key_rows + query_rows) // 8) * 8
    k_sum = jnp.sum(jnp.square(k_raw.astype(jnp.float32)), axis=1)
    q_sum = jnp.sum(jnp.square(q_raw.astype(jnp.float32)), axis=1)
    pad = (stat_rows - key_rows - query_rows) * HD
    stats = jnp.concatenate((k_sum, q_sum, jnp.zeros((pad,), jnp.float32))).reshape(stat_rows, HD)
    parts = [stats]
    for step in range(1, group_count):
        parts.append(
            lax.ppermute(
                stats, "head", [(i, (i + step) % group_count) for i in range(group_count)]
            )
        )

    q_row, k_row = q_gain.reshape(1, local_width), k_gain.reshape(1, local_width)
    far_shape = (slab_count, 2 * CAP, TILE, HD)
    outgoing = pl.pallas_call(
        functools.partial(gather_kernel, full_width, head_step, group_count),
        out_shape=array(far_shape),
        in_specs=[SMEM] + [VMEM] * group_count + [VMEM, HBM, HBM],
        out_specs=HBM,
        scratch_shapes=[
            pltpu.VMEM((slots, TILE, HD), jnp.bfloat16),
            pltpu.VMEM((slots, TILE, HD), jnp.bfloat16),
            pltpu.VMEM((slots, TILE, HD), jnp.bfloat16),
            pltpu.VMEM((key_tokens, HD), jnp.float32),
            pltpu.SemaphoreType.DMA((4, slots)),
        ],
        compiler_params=grant(62700000),
        name="gather_far",
    )(wanted, *parts, k_gain, k_raw, values)
    far = lax.all_to_all(outgoing, "slab", split_axis=0, concat_axis=0, tiled=True)

    near = kept_tiles[:, :, :NEAR] - own_slab * key_tiles
    tile_ids = jnp.arange(key_tiles, dtype=jnp.int32)
    kept = jnp.any(near[:, :, :, None] == tile_ids, axis=2)
    mask = jnp.where(kept, 0.0, MASKED).astype(jnp.float32).transpose(1, 2, 0)
    mask = jnp.repeat(mask, TILE, axis=2)

    def column(tokens):
        return pl.BlockSpec((tokens, HD), lambda h: (0, h))

    def each_head(*shape):
        return pl.BlockSpec((1, *shape), lambda h: (h,) + (0,) * len(shape))

    all_stats = pl.BlockSpec((stat_rows, HD), lambda h: (0, 0))
    gain_spec = pl.BlockSpec((1, HD), lambda h: (0, h))
    queries, keys = (query_tokens, local_width), (key_tokens, local_width)
    keys_h, queries_h = (head_count, key_tokens, HD), (head_count, query_tokens, HD)
    keys_t, queries_t = (head_count, HD, key_tokens), (head_count, HD, query_tokens)
    stat_shape = (head_count, 8, query_tokens)
    probs_shape = (head_count, key_tokens, query_tokens)
    far_ds_shape = (head_count, 2 * TILE, query_tokens)
    far_k_shape = (slab_count, CAP, TILE, HD)
    kn, qn, kn_t, v_t, cot_t, stat = pl.pallas_call(
        functools.partial(near_kernel, full_width, group_count),
        grid=(head_count,),
        in_specs=[all_stats] * group_count
        + [
            column(query_tokens),
            column(key_tokens),
            column(key_tokens),
            column(query_tokens),
            gain_spec,
            gain_spec,
            each_head(key_tiles, query_tokens),
        ],
        out_specs=[
            column(key_tokens),
            column(query_tokens),
            each_head(HD, key_tokens),
            each_head(HD, key_tokens),
            each_head(HD, query_tokens),
            each_head(8, query_tokens),
        ],
        out_shape=[
            array(keys),
            array(queries),
            array(keys_t),
            array(keys_t),
            array(queries_t),
            array(stat_shape, jnp.float32),
        ],
        scratch_shapes=[pltpu.VMEM((key_tokens, query_tokens), jnp.float32)],
        compiler_params=pltpu.CompilerParams(vmem_limit_bytes=60 << 20),
        name="near",
    )(*parts, q_raw, k_raw, values, cotangent, q_row, k_row, mask)

    attn_out, probs, delta, far_ds, far_k, far_grad = pl.pallas_call(
        functools.partial(meet_kernel, head_step),
        in_specs=[SMEM] * 2 + [HBM] * 8,
        out_specs=[HBM] * 6,
        out_shape=[
            array(queries),
            array(probs_shape),
            array(stat_shape, jnp.float32),
            array(far_ds_shape),
            array(far_k_shape),
            array(far_shape),
        ],
        scratch_shapes=[
            pltpu.VMEM(far_shape, jnp.bfloat16),
            pltpu.VMEM(keys_h, jnp.bfloat16),
            pltpu.VMEM(queries_h, jnp.bfloat16),
            pltpu.VMEM(stat_shape, jnp.float32),
            pltpu.VMEM((head_count, key_tiles, query_tokens), jnp.float32),
            pltpu.VMEM(keys_t, jnp.bfloat16),
            pltpu.VMEM(queries_t, jnp.bfloat16),
            pltpu.VMEM(queries_h, jnp.bfloat16),
            pltpu.VMEM(queries_h, jnp.bfloat16),
            pltpu.VMEM(probs_shape, jnp.bfloat16),
            pltpu.VMEM(stat_shape, jnp.float32),
            pltpu.VMEM(far_ds_shape, jnp.bfloat16),
            pltpu.VMEM(far_ds_shape, jnp.bfloat16),
            pltpu.VMEM((HD, query_tokens), jnp.float32),
            pltpu.VMEM(stat_shape, jnp.float32),
            pltpu.VMEM((slots, TILE, HD), jnp.float32),
            pltpu.VMEM((slots, TILE, HD), jnp.float32),
            pltpu.VMEM(far_shape, jnp.bfloat16),
            pltpu.SemaphoreType.DMA((head_count + 1, 7)),
            pltpu.SemaphoreType.DMA((head_count + 1, 4)),
        ],
        compiler_params=vmem,
        name="meet",
    )(kept_flat, request, kn, qn, stat, mask, v_t, cot_t, cotangent, far)
    back = lax.all_to_all(far_grad, "slab", split_axis=0, concat_axis=0, tiled=True)

    dq_normed, dk, dv, tiles = pl.pallas_call(
        functools.partial(grad_kernel, head_step),
        in_specs=[SMEM] * 3 + [HBM] * 8,
        out_specs=[HBM] * 4,
        out_shape=[
            array(queries),
            array(keys),
            array(keys),
            array((slots, TILE, 2 * HD), jnp.float32),
        ],
        scratch_shapes=[
            pltpu.VMEM(keys_t, jnp.bfloat16),
            pltpu.VMEM(queries, jnp.bfloat16),
            pltpu.VMEM(keys, jnp.bfloat16),
            pltpu.VMEM(queries, jnp.bfloat16),
            pltpu.VMEM((head_count, key_tokens, 2 * query_tokens), jnp.bfloat16),
            pltpu.VMEM(stat_shape, jnp.float32),
            pltpu.VMEM(far_ds_shape, jnp.bfloat16),
            pltpu.VMEM(far_k_shape, jnp.bfloat16),
            pltpu.VMEM((2, 2 * query_tokens, 2 * HD), jnp.bfloat16),
            pltpu.VMEM((head_count, key_tokens, 2 * HD), jnp.float32),
            pltpu.VMEM(queries, jnp.bfloat16),
            pltpu.VMEM(keys, jnp.bfloat16),
            pltpu.VMEM(keys, jnp.bfloat16),
            pltpu.SemaphoreType.DMA((head_count + 1, 7)),
            pltpu.SemaphoreType.DMA((head_count + 1, 2)),
            pltpu.SemaphoreType.DMA((slots,)),
        ],
        compiler_params=vmem,
        name="grad",
    )(kept_flat, request, wanted, kn_t, qn, values, cotangent, probs, delta, far_ds, far_k)

    dk, dv = pl.pallas_call(
        functools.partial(finish_kernel, head_step),
        out_shape=[array(keys), array(keys)],
        in_specs=[SMEM, ANYWHERE, HBM, HBM, HBM],
        out_specs=[HBM, HBM],
        scratch_shapes=[
            pltpu.VMEM(far_shape, jnp.bfloat16),
            pltpu.VMEM((slots, TILE, 2 * HD), jnp.float32),
            pltpu.VMEM((slots, TILE, HD), jnp.bfloat16),
            pltpu.VMEM((slots, TILE, HD), jnp.bfloat16),
            pltpu.SemaphoreType.DMA((3, slots)),
        ],
        input_output_aliases={3: 0, 4: 1},
        compiler_params=grant(50 << 20),
        name="finish",
    )(wanted, back, tiles, dk, dv)
    return attn_out, dq_normed, dk, dv


def solution(mesh):
    tokens = P("slab", "head")
    return jax.shard_map(
        local,
        mesh=mesh,
        in_specs=(tokens, tokens, tokens, P("head"), P("head"), tokens, P("slab", "head", None)),
        out_specs=(tokens, tokens, tokens, tokens),
        check_vma=False,
    )
```
